256 devices in a mesh: pipe: 16 (over x, z_hi, core), dp: 4 (over z_lo), mp: 4 (over y).
Axes of the slice: x: 4, y: 4, z: 8 (z_hi: 2, z_lo: 4; z = z_hi * 4 + z_lo), core: 2. Of those that a mesh axis runs over, the one named last changes fastest.
Arguments:
- layer_input: bfloat16 [16, 1024, 16384], P('pipe', 'dp', 'mp'), may hold values from -6 to 6
- kv_cotangent: bfloat16 [16, 1024, 2, 1024], P('pipe', 'dp', None, 'mp'), may hold values from -6 to 6
- kv_weight: bfloat16 [16, 16384, 2, 1024], P('pipe', 'dp', None, 'mp'), may hold values from -0.046875 to 0.046875
Outputs:
- input_grad: bfloat16 [16, 1024, 16384], P('pipe', None, ('dp', 'mp'))
- grad_mantissa: bfloat16 [16, 16384, 2, 1024], P('pipe', 'dp', None, 'mp')
- grad_scale: float32 [16, 16384, 2, 8], P('pipe', 'dp', None, 'mp')
The draws below stay inside these ranges and needn't reach their ends.
All inputs are finite; a program needn't handle non-finite values. Where the reference program divides by a largest or mean magnitude, that divisor is 1e-20 or more.
Results may differ from the reference program's by a relative error of at most 0.018.
Values may be sent and summed in bfloat16 or wider, within the bound.
A program may use at most 192 MiB of HBM per device.

```python
import jax
import jax.numpy as jnp
from jax import lax

D = 16384
KVH = 8
HD = 128
BLOCK = 128
TOK_DEV = 256
TOKENS = 1024
SECTIONS = 16
N_DP = 4


def strengthened(values, key, source, target, parts, factor):
    def block_of(axis_at):
        return (jnp.arange(values.shape[axis_at]) // (values.shape[axis_at] // parts)).reshape((-1,) + (1,) * (values.ndim - 1 - axis_at))

    first = jax.random.permutation(key, parts)[block_of(target)]
    other_side = (block_of(target) + parts // 2) % parts
    return jnp.where((block_of(source) == first) | (block_of(source) == other_side), factor * values, values)


def shard_levels(own_key, shape, shards, least, high):
    gain = 1.0
    for dim, shards_of in shards:
        heights = jax.random.uniform(jax.random.fold_in(jax.random.fold_in(own_key, 6), dim), (shards_of,), jnp.float32, least / len(shards), high / len(shards))
        gain = gain * jnp.repeat(jnp.exp(heights), shape[dim] // shards_of).reshape((-1,) + (1,) * (len(shape) - 1 - dim))
    return gain


def scatter_about(rng, extent, width, bound, pieces=(), dtype=jnp.bfloat16):
    gain = shard_levels(rng, extent, pieces, -0.22, 0.18) if pieces else 1.0
    entries = jax.random.normal(rng, extent, jnp.float32) * width * gain
    return jnp.minimum(jnp.maximum(entries, -bound), bound).astype(dtype)


def bell_draw_with(rng, shape, scale, most, cuts, heavy, kind=jnp.bfloat16):
    result = scale * jax.random.normal(rng, shape, jnp.float32)
    if cuts:
        result = result * shard_levels(rng, shape, cuts, -0.22, 0.18)
    return jnp.clip(strengthened(result, jax.random.fold_in(rng, 3), *heavy), -most, most).astype(kind)


def setup_inputs(seed: int = 0) -> dict:
    key_of = jax.random.split(jax.random.key(seed), 4)
    return {
        "layer_input": bell_draw_with(key_of[0], (SECTIONS, TOKENS, D), 1.0, 6.0, ((0, 16), (1, 4), (2, 4)), (1, 2, 4, 2.0)),
        "kv_cotangent": scatter_about(key_of[1], (SECTIONS, TOKENS, 2, KVH * HD), 1.0, 6.0, ((0, 16), (1, 4), (3, 4))),
        "kv_weight": scatter_about(key_of[2], (SECTIONS, D, 2, KVH * HD), D ** -0.5, 0.046875, ((0, 16), (1, 4), (3, 4))),
    }


def one_section(section_args):
    layer_input, kv_cotangent, kv_weight = section_args
    columns = 2 * KVH * HD
    flat_grad = kv_cotangent.reshape(TOKENS, columns)
    flat_weight = kv_weight.reshape(D, columns)
    produced = lax.dot_general(flat_grad, flat_weight, (((1,), (1,)), ((), ())), preferred_element_type=jnp.float32).astype(jnp.bfloat16)
    groups_in = layer_input.reshape(N_DP, TOK_DEV, D)
    groups_grad = flat_grad.reshape(N_DP, TOK_DEV, columns)

    def group_partial(pair):
        return lax.dot_general(pair[0], pair[1], (((0,), (0,)), ((), ())), preferred_element_type=jnp.float32)

    partial_value = lax.map(group_partial, (groups_in, groups_grad))
    blocked = partial_value.reshape(N_DP, D, columns // BLOCK, BLOCK)
    grad_scale = jnp.max(jnp.abs(blocked), axis=(0, 3)) + 1e-6
    terms = (blocked / grad_scale[None, :, :, None]).astype(jnp.bfloat16)
    terms = lax.optimization_barrier(terms).astype(jnp.float32)
    grad_mantissa = jnp.sum(terms, axis=0).astype(jnp.bfloat16).reshape(D, 2, KVH * HD)
    return produced, grad_mantissa, grad_scale.reshape(D, 2, KVH * HD // BLOCK)


def reference(layer_input, kv_cotangent, kv_weight):
    produced, grad_mantissa, grad_scale = lax.map(one_section, (layer_input, kv_cotangent, kv_weight))
    input_grad = jnp.concatenate([produced[1:], jnp.zeros_like(produced[:1])], axis=0)
    return input_grad, grad_mantissa, grad_scale
```

```python
import functools

import jax
import jax.numpy as jnp
from jax import lax
from jax.experimental import pallas as pl
from jax.experimental.pallas import tpu as pltpu
from jax.sharding import PartitionSpec as P

BLOCK = 128
TINY = 1e-6
MESH = pl.DeviceIdType.MESH
PARTS = 4


def wrap(index):
    return lax.rem(index + 2 * PARTS, PARTS)


def section_kernel(
    sections,
    x_ref,
    g_ref,
    w_ref,
    out_grad,
    out_mant,
    out_scale,
    x_stage,
    x_all,
    g_all,
    w_all,
    mant,
    scale,
    made,
    zeros,
    x_send,
    x_recv,
    xz_send,
    xz_recv,
    gz_send,
    gz_recv,
    gy_send,
    gy_recv,
    gf_send,
    gf_recv,
    w_send,
    w_recv,
    m_send,
    m_recv,
    s_send,
    s_recv,
    p_send,
    p_recv,
    local_sem,
    m_local,
    zero_sem,
):
    pipe, dp, mp = lax.axis_index("pipe"), lax.axis_index("dp"), lax.axis_index("mp")
    tokens, features = x_ref.shape
    columns = g_ref.shape[1]
    share = features // PARTS
    chunk = share // PARTS
    all_tokens = tokens * PARTS
    half = all_tokens // 2
    blocks = columns // BLOCK

    def along_mp(by):
        return (pipe, dp, wrap(mp + by))

    def along_dp(to):
        return (pipe, to, mp)

    def remote(src, dst, send, recv, device):
        return pltpu.make_async_remote_copy(
            src_ref=src, dst_ref=dst, send_sem=send, recv_sem=recv, device_id=device, device_id_type=MESH
        )

    barrier = pltpu.get_barrier_semaphore()
    for by in range(1, PARTS):
        pl.semaphore_signal(barrier, inc=1, device_id=along_mp(by), device_id_type=MESH)
        pl.semaphore_signal(barrier, inc=1, device_id=along_dp(wrap(dp + by)), device_id_type=MESH)

    for by in (1, sections - 1):
        pl.semaphore_signal(
            barrier, inc=1, device_id=(lax.rem(pipe + by, sections), dp, mp), device_id_type=MESH
        )
    pl.semaphore_wait(barrier, 2 * (PARTS - 1) + 2)

    def quarter(index):
        return pl.ds(pl.multiple_of(index * share, share), share)

    def token_rows(index):
        return pl.ds(pl.multiple_of(index * tokens, tokens), tokens)

    x_out = [
        remote(
            x_ref.at[:, quarter(wrap(mp + by))], x_stage.at[by], x_send.at[by], x_recv.at[by], along_mp(by)
        )
        for by in range(1, PARTS)
    ]
    for copy in x_out:
        copy.start()
    own_g = pltpu.make_async_copy(g_ref, g_all.at[0, token_rows(dp)], local_sem.at[0])
    own_w = pltpu.make_async_copy(w_ref.at[quarter(mp)], w_all.at[0], local_sem.at[1])
    own_g.start()
    gz_out = [
        remote(
            g_ref, g_all.at[0, token_rows(dp)], gz_send.at[by], gz_recv.at[by], along_dp(wrap(dp + by))
        )
        for by in range(1, PARTS)
    ]
    for copy in gz_out:
        copy.start()
    own_w.start()

    def x_from(by):
        return x_ref.at[:, quarter(mp)] if by == 0 else x_stage.at[by]

    def x_on(by):
        owner = wrap(mp - by)
        return remote(x_from(by), x_all.at[dp], xz_send.at[by], xz_recv.at[dp], along_dp(owner))

    for by in range(PARTS):
        if by > 0:
            x_out[by - 1].wait_recv()

        @pl.when(wrap(mp - by) != dp)
        def _():
            x_on(by).start()

        @pl.when(wrap(mp - by) == dp)
        def _():
            pltpu.make_async_copy(x_from(by), x_all.at[dp], local_sem.at[2]).start()

    own_g.wait()
    for by in range(1, PARTS):
        remote(
            g_ref, g_all.at[0, token_rows(wrap(dp - by))], gz_send.at[by], gz_recv.at[by], along_dp(wrap(dp + by))
        ).wait_recv()

    def g_half(slot, part):
        return g_all.at[slot, pl.ds(part * half, half)]

    def g_out(side, part):
        by, slot = (1, 1) if side == 0 else (-1, 3)
        return remote(
            g_half(0, part), g_half(slot, part), gy_send.at[side, part], gy_recv.at[side, part], along_mp(by)
        )

    def g_on(side):
        by, slot = (1, 1) if side == 0 else (-1, 3)
        return remote(g_half(slot, side), g_half(2, side), gf_send.at[side], gf_recv.at[side], along_mp(by))

    for part in range(2):
        g_out(0, part).start()
        g_out(1, 1 - part).start()

    def w_out(by, part):
        rows = pl.ds(pl.multiple_of(wrap(mp + by) * share + part * chunk, chunk), chunk)
        return remote(
            w_ref.at[rows],
            w_all.at[by, pl.ds(pl.multiple_of(part * chunk, chunk), chunk)],
            w_send.at[by, part],
            w_recv.at[by, part],
            along_mp(by),
        )

    for by in range(1, PARTS):
        w_out(by, 0).start()
    for side in range(2):
        g_out(side, side).wait_recv()
        g_on(side).start()
    for part in range(1, PARTS):
        for by in range(1, PARTS):
            w_out(by, part).start()

    @pl.when(pipe == sections - 1)
    def _():
        zeros[...] = jnp.zeros_like(zeros)
        for part in range(PARTS):
            pltpu.make_async_copy(
                zeros, out_grad.at[pl.ds(part * tokens, tokens)], zero_sem.at[part]
            ).start()

    for side in range(2):
        g_out(side, 1 - side).wait_recv()
        g_on(side).wait_recv()
    for by in range(1, PARTS):
        source = wrap(dp - by)
        remote(x_stage.at[0], x_all.at[source], xz_send.at[0], xz_recv.at[source], along_dp(source)).wait_recv()
    pltpu.make_async_copy(x_stage.at[0], x_all.at[dp], local_sem.at[2]).wait()

    def m_out(turn, part):
        rows = pl.ds(pl.multiple_of(mp * share + part * chunk, chunk), chunk)
        src = mant.at[turn, pl.ds(pl.multiple_of(part * chunk, chunk), chunk)]
        return remote(src, out_mant.at[rows], m_send.at[turn, part], m_recv.at[turn, part], along_mp(1 + turn))

    def m_here(part):
        rows = pl.ds(pl.multiple_of(mp * share + part * chunk, chunk), chunk)
        src = mant.at[PARTS - 1, pl.ds(pl.multiple_of(part * chunk, chunk), chunk)]
        return pltpu.make_async_copy(src, out_mant.at[rows], m_local.at[part])

    def weight_step(step, _):
        turn, part = step // PARTS, lax.rem(step, PARTS)
        slot = PARTS - 1 - turn
        rows = pl.ds(pl.multiple_of(part * chunk, chunk), chunk)
        partial = [
            lax.dot_general(
                x_all[group, :, rows],
                g_all[slot, pl.ds(group * tokens, tokens), :],
                (((0,), (0,)), ((), ())),
                preferred_element_type=jnp.float32,
            )
            for group in range(PARTS)
        ]
        largest = jnp.abs(partial[0])
        for group in range(1, PARTS):
            largest = jnp.maximum(largest, jnp.abs(partial[group]))
        lanes = lax.broadcasted_iota(jnp.int32, (chunk, BLOCK), 1)
        gathered = jnp.zeros((chunk, BLOCK), jnp.float32)
        for block in range(blocks):
            cols = slice(block * BLOCK, (block + 1) * BLOCK)
            size = jnp.max(largest[:, cols], axis=1, keepdims=True) + TINY
            gathered = jnp.where(lanes == block, size, gathered)
            inverse = 1.0 / size
            total = None
            for group in range(PARTS):
                term = (partial[group][:, cols] * inverse).astype(jnp.bfloat16).astype(jnp.float32)
                total = term if total is None else total + term
            mant[turn, rows, cols] = total.astype(jnp.bfloat16)
        scale[turn, :, rows] = jnp.transpose(gathered)[:8, :]

        @pl.when(turn < PARTS - 1)
        def _():
            m_out(turn, part).start()

        @pl.when(turn == PARTS - 1)
        def _():
            m_here(part).start()

        return 0

    lax.fori_loop(0, PARTS * PARTS, weight_step, 0)

    def s_out(turn):
        cols = pl.ds(pl.multiple_of(mp * share, share), share)
        return remote(scale.at[turn], out_scale.at[:, cols], s_send.at[turn], s_recv.at[turn], along_mp(1 + turn))

    for turn in range(PARTS - 1):
        s_out(turn).start()
    s_here = pltpu.make_async_copy(
        scale.at[PARTS - 1], out_scale.at[:, pl.ds(pl.multiple_of(mp * share, share), share)], local_sem.at[3]
    )
    s_here.start()

    def p_out(part):
        cols = pl.ds(pl.multiple_of(part * chunk, chunk), chunk)
        before = jnp.maximum(pipe - 1, 0)
        return remote(
            made.at[:, cols], out_grad.at[:, cols], p_send.at[part], p_recv.at[part], (before, dp, mp)
        )

    own_w.wait()

    def input_step(part, _):
        for by in range(1, PARTS):
            w_out(by, part).wait_recv()
        rows = pl.ds(pl.multiple_of(part * chunk, chunk), chunk)

        def token_step(group, _):
            own = pl.ds(pl.multiple_of(group * tokens, tokens), tokens)
            total = None
            for slot in range(PARTS):
                term = lax.dot_general(
                    g_all[slot, own, :],
                    w_all[slot, rows, :],
                    (((1,), (1,)), ((), ())),
                    preferred_element_type=jnp.float32,
                )
                total = term if total is None else total + term
            made[own, rows] = total.astype(jnp.bfloat16)
            return 0

        lax.fori_loop(0, PARTS, token_step, 0)

        @pl.when(pipe > 0)
        def _():
            p_out(part).start()

        return 0

    lax.fori_loop(0, PARTS, input_step, 0)

    for copy in x_out + gz_out:
        copy.wait_send()
    for by in range(PARTS):

        @pl.when(wrap(mp - by) != dp)
        def _():
            x_on(by).wait_send()

    for side in range(2):
        for part in range(2):
            g_out(side, part).wait_send()
        g_on(side).wait_send()
    for by in range(1, PARTS):
        for part in range(PARTS):
            w_out(by, part).wait_send()
    for turn in range(PARTS - 1):
        source = wrap(mp - 1 - turn)
        for part in range(PARTS):
            m_out(turn, part).wait_send()
            rows = pl.ds(pl.multiple_of(source * share + part * chunk, chunk), chunk)
            remote(
                mant.at[turn, pl.ds(part * chunk, chunk)],
                out_mant.at[rows],
                m_send.at[turn, part],
                m_recv.at[turn, part],
                along_mp(1 + turn),
            ).wait_recv()
        s_out(turn).wait_send()
        cols = pl.ds(pl.multiple_of(source * share, share), share)
        remote(
            scale.at[turn], out_scale.at[:, cols], s_send.at[turn], s_recv.at[turn], along_mp(1 + turn)
        ).wait_recv()
    for part in range(PARTS):
        m_here(part).wait()
    s_here.wait()

    @pl.when(pipe > 0)
    def _():
        for part in range(PARTS):
            p_out(part).wait_send()

    @pl.when(pipe < sections - 1)
    def _():
        for part in range(PARTS):
            p_out(part).wait_recv()

    @pl.when(pipe == sections - 1)
    def _():
        for part in range(PARTS):
            pltpu.make_async_copy(
                zeros, out_grad.at[pl.ds(part * tokens, tokens)], zero_sem.at[part]
            ).wait()


def on_device(sections, layer_input, kv_cotangent, kv_weight):
    features = layer_input[0]
    tokens, width = features.shape
    columns = 2 * kv_cotangent.shape[3]
    rows = kv_weight.shape[1]
    flat_grad = kv_cotangent.reshape(tokens, columns)
    flat_weight = kv_weight.reshape(rows, columns)
    share = width // PARTS
    blocks = columns // BLOCK
    dma = pltpu.SemaphoreType.DMA
    anywhere = pl.BlockSpec(memory_space=pl.ANY)
    grad, mantissa, scale = pl.pallas_call(
        functools.partial(section_kernel, sections),
        out_shape=(
            jax.ShapeDtypeStruct((tokens * PARTS, share), jnp.bfloat16),
            jax.ShapeDtypeStruct((rows, columns), jnp.bfloat16),
            jax.ShapeDtypeStruct((8, rows), jnp.float32),
        ),
        in_specs=[anywhere] * 3,
        out_specs=[anywhere] * 3,
        scratch_shapes=[
            pltpu.VMEM((PARTS, tokens, share), jnp.bfloat16),
            pltpu.VMEM((PARTS, tokens, share), jnp.bfloat16),
            pltpu.VMEM((PARTS, tokens * PARTS, columns), jnp.bfloat16),
            pltpu.VMEM((PARTS, share, columns), jnp.bfloat16),
            pltpu.VMEM((PARTS, share, columns), jnp.bfloat16),
            pltpu.VMEM((PARTS, 8, share), jnp.float32),
            pltpu.VMEM((tokens * PARTS, share), jnp.bfloat16),
            pltpu.VMEM((tokens, share), jnp.bfloat16),
            dma((PARTS,)),
            dma((PARTS,)),
            dma((PARTS,)),
            dma((PARTS,)),
            dma((PARTS,)),
            dma((PARTS,)),
            dma((2, 2)),
            dma((2, 2)),
            dma((2,)),
            dma((2,)),
            dma((PARTS, PARTS)),
            dma((PARTS, PARTS)),
            dma((PARTS, PARTS)),
            dma((PARTS, PARTS)),
            dma((PARTS,)),
            dma((PARTS,)),
            dma((PARTS,)),
            dma((PARTS,)),
            dma((4,)),
            dma((PARTS,)),
            dma((PARTS,)),
        ],
        name="section",
        compiler_params=pltpu.CompilerParams(
            collective_id=0, has_side_effects=True, vmem_limit_bytes=48 << 20
        ),
    )(features, flat_grad, flat_weight)
    mantissa = mantissa.reshape(rows, 2, columns // 2)
    scale = scale[:blocks].T.reshape(rows, 2, blocks // 2)
    return grad[None], mantissa[None], scale[None]


def solution(mesh):
    in_specs = (P("pipe", "dp", "mp"), P("pipe", "dp", None, "mp"), P("pipe", "dp", None, "mp"))
    out_specs = (
        P("pipe", None, ("dp", "mp")),
        P("pipe", "dp", None, "mp"),
        P("pipe", "dp", None, "mp"),
    )
    return jax.shard_map(
        functools.partial(on_device, mesh.shape["pipe"]),
        mesh=mesh,
        in_specs=in_specs,
        out_specs=out_specs,
        check_vma=False,
    )
```

```python
import functools

import jax
import jax.numpy as jnp
from jax import lax
from jax.experimental import pallas as pl
from jax.experimental.pallas import tpu as pltpu
from jax.sharding import PartitionSpec as P

BLOCK = 128
TINY = 1e-6
MESH = pl.DeviceIdType.MESH
PARTS = 4


def wrap(index):
    return lax.rem(index + 2 * PARTS, PARTS)


def section_kernel(
    sections,
    x_ref,
    g_ref,
    w_ref,
    out_grad,
    out_mant,
    out_scale,
    x_stage,
    x_all,
    g_all,
    w_all,
    mant,
    scale,
    made,
    zeros,
    x_send,
    x_recv,
    xz_send,
    xz_recv,
    gz_send,
    gz_recv,
    gy_send,
    gy_recv,
    gf_send,
    gf_recv,
    w_send,
    w_recv,
    m_send,
    m_recv,
    s_send,
    s_recv,
    p_send,
    p_recv,
    local_sem,
    m_local,
    zero_sem,
):
    pipe, dp, mp = lax.axis_index("pipe"), lax.axis_index("dp"), lax.axis_index("mp")
    tokens, features = x_ref.shape
    columns = g_ref.shape[1]
    share = features // PARTS
    chunk = share // PARTS
    all_tokens = tokens * PARTS
    half = all_tokens // 2
    blocks = columns // BLOCK

    def along_mp(by):
        return (pipe, dp, wrap(mp + by))

    def along_dp(to):
        return (pipe, to, mp)

    def remote(src, dst, send, recv, device):
        return pltpu.make_async_remote_copy(
            src_ref=src, dst_ref=dst, send_sem=send, recv_sem=recv, device_id=device, device_id_type=MESH
        )

    barrier = pltpu.get_barrier_semaphore()
    for by in range(1, PARTS):
        pl.semaphore_signal(barrier, inc=1, device_id=along_mp(by), device_id_type=MESH)
        pl.semaphore_signal(barrier, inc=1, device_id=along_dp(wrap(dp + by)), device_id_type=MESH)

    for by in (1, sections - 1):
        pl.semaphore_signal(
            barrier, inc=1, device_id=(lax.rem(pipe + by, sections), dp, mp), device_id_type=MESH
        )
    pl.semaphore_wait(barrier, 2 * (PARTS - 1) + 2)

    def quarter(index):
        return pl.ds(pl.multiple_of(index * share, share), share)

    def token_rows(index):
        return pl.ds(pl.multiple_of(index * tokens, tokens), tokens)

    x_out = [
        remote(
            x_ref.at[:, quarter(wrap(mp + by))], x_stage.at[by], x_send.at[by], x_recv.at[by], along_mp(by)
        )
        for by in range(1, PARTS)
    ]
    for copy in x_out:
        copy.start()
    own_g = pltpu.make_async_copy(g_ref, g_all.at[0, token_rows(dp)], local_sem.at[0])
    own_w = pltpu.make_async_copy(w_ref.at[quarter(mp)], w_all.at[0], local_sem.at[1])
    own_g.start()
    gz_out = [
        remote(
            g_ref, g_all.at[0, token_rows(dp)], gz_send.at[by], gz_recv.at[by], along_dp(wrap(dp + by))
        )
        for by in range(1, PARTS)
    ]
    for copy in gz_out:
        copy.start()
    own_w.start()

    def x_from(by):
        return x_ref.at[:, quarter(mp)] if by == 0 else x_stage.at[by]

    def x_on(by):
        owner = wrap(mp - by)
        return remote(x_from(by), x_all.at[dp], xz_send.at[by], xz_recv.at[dp], along_dp(owner))

    for by in range(PARTS):
        if by > 0:
            x_out[by - 1].wait_recv()

        @pl.when(wrap(mp - by) != dp)
        def _():
            x_on(by).start()

        @pl.when(wrap(mp - by) == dp)
        def _():
            pltpu.make_async_copy(x_from(by), x_all.at[dp], local_sem.at[2]).start()

    def w_out(by, part):
        rows = pl.ds(pl.multiple_of(wrap(mp + by) * share + part * chunk, chunk), chunk)
        return remote(
            w_ref.at[rows],
            w_all.at[by, pl.ds(pl.multiple_of(part * chunk, chunk), chunk)],
            w_send.at[by, part],
            w_recv.at[by, part],
            along_mp(by),
        )

    for part in range(PARTS // 2):
        for by in range(1, PARTS):
            w_out(by, part).start()

    own_g.wait()
    for by in range(1, PARTS):
        remote(
            g_ref, g_all.at[0, token_rows(wrap(dp - by))], gz_send.at[by], gz_recv.at[by], along_dp(wrap(dp + by))
        ).wait_recv()

    def g_half(slot, part):
        return g_all.at[slot, pl.ds(part * half, half)]

    def g_out(side, part):
        by, slot = (1, 1) if side == 0 else (-1, 3)
        return remote(
            g_half(0, part), g_half(slot, part), gy_send.at[side, part], gy_recv.at[side, part], along_mp(by)
        )

    def g_on(side):
        by, slot = (1, 1) if side == 0 else (-1, 3)
        return remote(g_half(slot, side), g_half(2, side), gf_send.at[side], gf_recv.at[side], along_mp(by))

    for part in range(2):
        g_out(0, part).start()
        g_out(1, 1 - part).start()

    for side in range(2):
        g_out(side, side).wait_recv()
        g_on(side).start()
    for part in range(PARTS // 2, PARTS):
        for by in range(1, PARTS):
            w_out(by, part).start()

    @pl.when(pipe == sections - 1)
    def _():
        zeros[...] = jnp.zeros_like(zeros)
        for part in range(PARTS):
            pltpu.make_async_copy(
                zeros, out_grad.at[pl.ds(part * tokens, tokens)], zero_sem.at[part]
            ).start()

    for side in range(2):
        g_out(side, 1 - side).wait_recv()
        g_on(side).wait_recv()
    def p_out(part):
        cols = pl.ds(pl.multiple_of(part * chunk, chunk), chunk)
        before = jnp.maximum(pipe - 1, 0)
        return remote(
            made.at[:, cols], out_grad.at[:, cols], p_send.at[part], p_recv.at[part], (before, dp, mp)
        )

    own_w.wait()

    def input_step(part, _):
        for by in range(1, PARTS):
            w_out(by, part).wait_recv()
        rows = pl.ds(pl.multiple_of(part * chunk, chunk), chunk)

        def token_step(group, _):
            own = pl.ds(pl.multiple_of(group * tokens, tokens), tokens)
            total = None
            for slot in range(PARTS):
                term = lax.dot_general(
                    g_all[slot, own, :],
                    w_all[slot, rows, :],
                    (((1,), (1,)), ((), ())),
                    preferred_element_type=jnp.float32,
                )
                total = term if total is None else total + term
            made[own, rows] = total.astype(jnp.bfloat16)
            return 0

        lax.fori_loop(0, PARTS, token_step, 0)

        @pl.when(pipe > 0)
        def _():
            p_out(part).start()

        return 0

    lax.fori_loop(0, PARTS // 2, input_step, 0)

    for by in range(1, PARTS):
        source = wrap(dp - by)
        remote(x_stage.at[0], x_all.at[source], xz_send.at[0], xz_recv.at[source], along_dp(source)).wait_recv()
    pltpu.make_async_copy(x_stage.at[0], x_all.at[dp], local_sem.at[2]).wait()

    def m_out(turn, part):
        rows = pl.ds(pl.multiple_of(mp * share + part * chunk, chunk), chunk)
        src = mant.at[turn, pl.ds(pl.multiple_of(part * chunk, chunk), chunk)]
        return remote(src, out_mant.at[rows], m_send.at[turn, part], m_recv.at[turn, part], along_mp(1 + turn))

    def m_here(part):
        rows = pl.ds(pl.multiple_of(mp * share + part * chunk, chunk), chunk)
        src = mant.at[PARTS - 1, pl.ds(pl.multiple_of(part * chunk, chunk), chunk)]
        return pltpu.make_async_copy(src, out_mant.at[rows], m_local.at[part])

    def weight_step(step, _):
        turn, part = step // PARTS, lax.rem(step, PARTS)
        slot = PARTS - 1 - turn
        rows = pl.ds(pl.multiple_of(part * chunk, chunk), chunk)
        partial = [
            lax.dot_general(
                x_all[group, :, rows],
                g_all[slot, pl.ds(group * tokens, tokens), :],
                (((0,), (0,)), ((), ())),
                preferred_element_type=jnp.float32,
            )
            for group in range(PARTS)
        ]
        largest = jnp.abs(partial[0])
        for group in range(1, PARTS):
            largest = jnp.maximum(largest, jnp.abs(partial[group]))
        lanes = lax.broadcasted_iota(jnp.int32, (chunk, BLOCK), 1)
        gathered = jnp.zeros((chunk, BLOCK), jnp.float32)
        for block in range(blocks):
            cols = slice(block * BLOCK, (block + 1) * BLOCK)
            size = jnp.max(largest[:, cols], axis=1, keepdims=True) + TINY
            gathered = jnp.where(lanes == block, size, gathered)
            inverse = 1.0 / size
            total = None
            for group in range(PARTS):
                term = (partial[group][:, cols] * inverse).astype(jnp.bfloat16).astype(jnp.float32)
                total = term if total is None else total + term
            mant[turn, rows, cols] = total.astype(jnp.bfloat16)
        scale[turn, :, rows] = jnp.transpose(gathered)[:8, :]

        @pl.when(turn < PARTS - 1)
        def _():
            m_out(turn, part).start()

        @pl.when(turn == PARTS - 1)
        def _():
            m_here(part).start()

        return 0

    lax.fori_loop(0, PARTS * PARTS, weight_step, 0)

    def s_out(turn):
        cols = pl.ds(pl.multiple_of(mp * share, share), share)
        return remote(scale.at[turn], out_scale.at[:, cols], s_send.at[turn], s_recv.at[turn], along_mp(1 + turn))

    for turn in range(PARTS - 1):
        s_out(turn).start()
    s_here = pltpu.make_async_copy(
        scale.at[PARTS - 1], out_scale.at[:, pl.ds(pl.multiple_of(mp * share, share), share)], local_sem.at[3]
    )
    s_here.start()

    lax.fori_loop(PARTS // 2, PARTS, input_step, 0)

    for copy in x_out + gz_out:
        copy.wait_send()
    for by in range(PARTS):

        @pl.when(wrap(mp - by) != dp)
        def _():
            x_on(by).wait_send()

    for side in range(2):
        for part in range(2):
            g_out(side, part).wait_send()
        g_on(side).wait_send()
    for by in range(1, PARTS):
        for part in range(PARTS):
            w_out(by, part).wait_send()
    for turn in range(PARTS - 1):
        source = wrap(mp - 1 - turn)
        for part in range(PARTS):
            m_out(turn, part).wait_send()
            rows = pl.ds(pl.multiple_of(source * share + part * chunk, chunk), chunk)
            remote(
                mant.at[turn, pl.ds(part * chunk, chunk)],
                out_mant.at[rows],
                m_send.at[turn, part],
                m_recv.at[turn, part],
                along_mp(1 + turn),
            ).wait_recv()
        s_out(turn).wait_send()
        cols = pl.ds(pl.multiple_of(source * share, share), share)
        remote(
            scale.at[turn], out_scale.at[:, cols], s_send.at[turn], s_recv.at[turn], along_mp(1 + turn)
        ).wait_recv()
    for part in range(PARTS):
        m_here(part).wait()
    s_here.wait()

    @pl.when(pipe > 0)
    def _():
        for part in range(PARTS):
            p_out(part).wait_send()

    @pl.when(pipe < sections - 1)
    def _():
        for part in range(PARTS):
            p_out(part).wait_recv()

    @pl.when(pipe == sections - 1)
    def _():
        for part in range(PARTS):
            pltpu.make_async_copy(
                zeros, out_grad.at[pl.ds(part * tokens, tokens)], zero_sem.at[part]
            ).wait()


def on_device(sections, layer_input, kv_cotangent, kv_weight):
    features = layer_input[0]
    tokens, width = features.shape
    columns = 2 * kv_cotangent.shape[3]
    rows = kv_weight.shape[1]
    flat_grad = kv_cotangent.reshape(tokens, columns)
    flat_weight = kv_weight.reshape(rows, columns)
    share = width // PARTS
    blocks = columns // BLOCK
    dma = pltpu.SemaphoreType.DMA
    anywhere = pl.BlockSpec(memory_space=pl.ANY)
    grad, mantissa, scale = pl.pallas_call(
        functools.partial(section_kernel, sections),
        out_shape=(
            jax.ShapeDtypeStruct((tokens * PARTS, share), jnp.bfloat16),
            jax.ShapeDtypeStruct((rows, columns), jnp.bfloat16),
            jax.ShapeDtypeStruct((8, rows), jnp.float32),
        ),
        in_specs=[anywhere] * 3,
        out_specs=[anywhere] * 3,
        scratch_shapes=[
            pltpu.VMEM((PARTS, tokens, share), jnp.bfloat16),
            pltpu.VMEM((PARTS, tokens, share), jnp.bfloat16),
            pltpu.VMEM((PARTS, tokens * PARTS, columns), jnp.bfloat16),
            pltpu.VMEM((PARTS, share, columns), jnp.bfloat16),
            pltpu.VMEM((PARTS, share, columns), jnp.bfloat16),
            pltpu.VMEM((PARTS, 8, share), jnp.float32),
            pltpu.VMEM((tokens * PARTS, share), jnp.bfloat16),
            pltpu.VMEM((tokens, share), jnp.bfloat16),
            dma((PARTS,)),
            dma((PARTS,)),
            dma((PARTS,)),
            dma((PARTS,)),
            dma((PARTS,)),
            dma((PARTS,)),
            dma((2, 2)),
            dma((2, 2)),
            dma((2,)),
            dma((2,)),
            dma((PARTS, PARTS)),
            dma((PARTS, PARTS)),
            dma((PARTS, PARTS)),
            dma((PARTS, PARTS)),
            dma((PARTS,)),
            dma((PARTS,)),
            dma((PARTS,)),
            dma((PARTS,)),
            dma((4,)),
            dma((PARTS,)),
            dma((PARTS,)),
        ],
        name="section",
        compiler_params=pltpu.CompilerParams(
            collective_id=0, has_side_effects=True, vmem_limit_bytes=48 << 20
        ),
    )(features, flat_grad, flat_weight)
    mantissa = mantissa.reshape(rows, 2, columns // 2)
    scale = scale[:blocks].T.reshape(rows, 2, blocks // 2)
    return grad[None], mantissa[None], scale[None]


def solution(mesh):
    in_specs = (P("pipe", "dp", "mp"), P("pipe", "dp", None, "mp"), P("pipe", "dp", None, "mp"))
    out_specs = (
        P("pipe", None, ("dp", "mp")),
        P("pipe", "dp", None, "mp"),
        P("pipe", "dp", None, "mp"),
    )
    return jax.shard_map(
        functools.partial(on_device, mesh.shape["pipe"]),
        mesh=mesh,
        in_specs=in_specs,
        out_specs=out_specs,
        check_vma=False,
    )
```

```python
import functools

import jax
import jax.numpy as jnp
from jax import lax
from jax.experimental import pallas as pl
from jax.experimental.pallas import tpu as pltpu
from jax.sharding import PartitionSpec as P

BLOCK = 128
SIDE = 256
EARLY = 3
TINY = 1e-6
MESH = pl.DeviceIdType.MESH
PARTS = 4


def wrap(index):
    return lax.rem(index + 2 * PARTS, PARTS)


def section_kernel(
    sections,
    x_ref,
    g_ref,
    w_ref,
    out_grad,
    out_mant,
    out_scale,
    x_stage,
    x_all,
    g_raw,
    g_own,
    w_raw,
    w_own,
    spread,
    gather,
    g_all,
    w_all,
    mant,
    scale,
    made,
    zeros,
    x_send,
    x_recv,
    xz_send,
    xz_recv,
    gz_send,
    gz_recv,
    gy_send,
    gy_recv,
    gf_send,
    gf_recv,
    gl_send,
    gl_recv,
    gn_send,
    gn_recv,
    w_send,
    w_recv,
    m_send,
    m_recv,
    s_send,
    s_recv,
    p_send,
    p_recv,
    local_sem,
    m_local,
    zero_sem,
):
    pipe, dp, mp = lax.axis_index("pipe"), lax.axis_index("dp"), lax.axis_index("mp")
    tokens, features = x_ref.shape
    columns = g_own.shape[1]
    share = features // PARTS
    chunk = share // PARTS
    lead = tokens * 3 // 4
    first, last = pl.ds(0, lead), pl.ds(lead, tokens - lead)
    blocks = columns // BLOCK
    step = SIDE // blocks

    def along_mp(by):
        return (pipe, dp, wrap(mp + by))

    def along_dp(to):
        return (pipe, to, mp)

    def remote(src, dst, send, recv, device):
        return pltpu.make_async_remote_copy(
            src_ref=src, dst_ref=dst, send_sem=send, recv_sem=recv, device_id=device, device_id_type=MESH
        )

    g_in = pltpu.make_async_copy(g_ref, g_raw, local_sem.at[4])
    w_in = pltpu.make_async_copy(w_ref, w_raw, local_sem.at[5])
    g_in.start()
    w_in.start()

    barrier = pltpu.get_barrier_semaphore()
    for by in range(1, PARTS):
        pl.semaphore_signal(barrier, inc=1, device_id=along_mp(by), device_id_type=MESH)
        pl.semaphore_signal(barrier, inc=1, device_id=along_dp(wrap(dp + by)), device_id_type=MESH)

    for by in (1, sections - 1):
        pl.semaphore_signal(
            barrier, inc=1, device_id=(lax.rem(pipe + by, sections), dp, mp), device_id_type=MESH
        )

    line = lax.broadcasted_iota(jnp.int32, (SIDE, SIDE), 0)
    column = lax.broadcasted_iota(jnp.int32, (SIDE, SIDE), 1)

    def place(index):
        return (index % 2 * 2 + index // 2 % 2) * step + index // blocks

    spread[...] = jnp.where(column == place(line), 1.0, 0.0).astype(jnp.bfloat16)
    gather[...] = jnp.where(line == place(column), 1.0, 0.0).astype(jnp.bfloat16)

    def untangle(raw, own, index):
        many = pl.ds(pl.multiple_of(index * SIDE, SIDE), SIDE)
        rows = pl.ds(pl.multiple_of(index * step, step), step)
        sorted_rows = jnp.dot(gather[...], raw[many, :], preferred_element_type=jnp.float32)
        for block in range(blocks):
            own[rows, block * BLOCK : (block + 1) * BLOCK] = sorted_rows[
                block * step : (block + 1) * step
            ].astype(jnp.bfloat16)

    g_in.wait()
    for index in range(tokens // step):
        untangle(g_raw, g_own, index)

    pl.semaphore_wait(barrier, 2 * (PARTS - 1) + 2)

    def quarter(index):
        return pl.ds(pl.multiple_of(index * share, share), share)

    x_out = [
        remote(
            x_ref.at[:, quarter(wrap(mp + by))], x_stage.at[by], x_send.at[by], x_recv.at[by], along_mp(by)
        )
        for by in range(1, PARTS)
    ]
    gl_out = [
        remote(g_own.at[last], g_all.at[by, dp, last], gl_send.at[by], gl_recv.at[by], along_mp(by))
        for by in range(1, PARTS)
    ]

    def gn_copy(by, block):
        part = g_all.at[:, block, last]
        return remote(part, part, gn_send.at[by], gn_recv.at[by], along_dp(wrap(dp + by)))

    for copy in gl_out:
        copy.start()
    for copy in x_out:
        copy.start()
    own_g = pltpu.make_async_copy(g_own, g_all.at[0, dp], local_sem.at[0])
    own_w = pltpu.make_async_copy(w_own.at[quarter(mp)], w_all.at[0], local_sem.at[1])
    own_g.start()
    gz_out = [
        remote(
            g_own.at[first], g_all.at[0, dp, first], gz_send.at[by], gz_recv.at[by], along_dp(wrap(dp + by))
        )
        for by in range(1, PARTS)
    ]
    for copy in gz_out:
        copy.start()

    own_g.wait()
    for copy in gl_out:
        copy.wait_recv()
    for by in range(1, PARTS):
        gn_copy(by, dp).start()
    w_in.wait()

    def untangle_weights(index, _):
        for part in range(PARTS):
            untangle(w_raw, w_own, index * PARTS + part)
        return 0

    lax.fori_loop(0, share // step, untangle_weights, 0)
    own_w.start()

    def x_from(by):
        return x_ref.at[:, quarter(mp)] if by == 0 else x_stage.at[by]

    def x_on(by):
        owner = wrap(mp - by)
        return remote(x_from(by), x_all.at[dp], xz_send.at[by], xz_recv.at[dp], along_dp(owner))

    for by in range(PARTS):
        if by > 0:
            x_out[by - 1].wait_recv()

        @pl.when(wrap(mp - by) != dp)
        def _():
            x_on(by).start()

        @pl.when(wrap(mp - by) == dp)
        def _():
            pltpu.make_async_copy(x_from(by), x_all.at[dp], local_sem.at[2]).start()

    def w_out(by, part):
        rows = pl.ds(pl.multiple_of(wrap(mp + by) * share + part * chunk, chunk), chunk)
        return remote(
            w_own.at[rows],
            w_all.at[by, pl.ds(pl.multiple_of(part * chunk, chunk), chunk)],
            w_send.at[by, part],
            w_recv.at[by, part],
            along_mp(by),
        )

    for part in range(EARLY):
        for by in range(1, PARTS):
            w_out(by, part).start()

    for by in range(1, PARTS):
        remote(
            g_own.at[first], g_all.at[0, wrap(dp - by), first], gz_send.at[by], gz_recv.at[by], along_dp(wrap(dp + by))
        ).wait_recv()

    def g_half(slot, part):
        return g_all.at[slot, pl.ds(part * (PARTS // 2), PARTS // 2), first]

    def g_out(side, part):
        by, slot = (1, 1) if side == 0 else (-1, 3)
        return remote(
            g_half(0, part), g_half(slot, part), gy_send.at[side, part], gy_recv.at[side, part], along_mp(by)
        )

    def g_on(side):
        by, slot = (1, 1) if side == 0 else (-1, 3)
        return remote(g_half(slot, side), g_half(2, side), gf_send.at[side], gf_recv.at[side], along_mp(by))

    for part in range(2):
        g_out(0, part).start()
        g_out(1, 1 - part).start()

    for side in range(2):
        g_out(side, side).wait_recv()
        g_on(side).start()
    for part in range(EARLY, PARTS):
        for by in range(1, PARTS):
            w_out(by, part).start()

    @pl.when(pipe == sections - 1)
    def _():
        zeros[...] = jnp.zeros_like(zeros)
        for part in range(PARTS):
            pltpu.make_async_copy(
                zeros, out_grad.at[pl.ds(part * tokens, tokens)], zero_sem.at[part]
            ).start()

    for side in range(2):
        g_out(side, 1 - side).wait_recv()
        g_on(side).wait_recv()
    for by in range(1, PARTS):
        gn_copy(by, wrap(dp - by)).wait_recv()
    def p_out(part):
        cols = pl.ds(pl.multiple_of(part * chunk, chunk), chunk)
        before = jnp.maximum(pipe - 1, 0)
        return remote(
            made.at[:, cols], out_grad.at[:, cols], p_send.at[part], p_recv.at[part], (before, dp, mp)
        )

    own_w.wait()

    def input_step(part, _):
        for by in range(1, PARTS):
            w_out(by, part).wait_recv()
        rows = pl.ds(pl.multiple_of(part * chunk, chunk), chunk)

        def token_step(group, _):
            own = pl.ds(pl.multiple_of(group * tokens, tokens), tokens)
            total = None
            for slot in range(PARTS):
                term = lax.dot_general(
                    g_all[slot, group],
                    w_all[slot, rows, :],
                    (((1,), (1,)), ((), ())),
                    preferred_element_type=jnp.float32,
                )
                total = term if total is None else total + term
            made[own, rows] = total.astype(jnp.bfloat16)
            return 0

        lax.fori_loop(0, PARTS, token_step, 0)

        @pl.when(pipe > 0)
        def _():
            p_out(part).start()

        return 0

    lax.fori_loop(0, PARTS // 2, input_step, 0)

    for by in range(1, PARTS):
        source = wrap(dp - by)
        remote(x_stage.at[0], x_all.at[source], xz_send.at[0], xz_recv.at[source], along_dp(source)).wait_recv()
    pltpu.make_async_copy(x_stage.at[0], x_all.at[dp], local_sem.at[2]).wait()

    def wide(first, size):
        return pl.ds(pl.multiple_of(first * blocks, size * blocks), size * blocks)

    def m_out(turn, part):
        rows = wide(mp * share + part * chunk, chunk)
        src = mant.at[turn, wide(part * chunk, chunk)]
        return remote(src, out_mant.at[rows], m_send.at[turn, part], m_recv.at[turn, part], along_mp(1 + turn))

    def m_here(part):
        rows = wide(mp * share + part * chunk, chunk)
        src = mant.at[PARTS - 1, wide(part * chunk, chunk)]
        return pltpu.make_async_copy(src, out_mant.at[rows], m_local.at[part])

    def weight_step(count, _):
        turn, part = count // PARTS, lax.rem(count, PARTS)
        slot = PARTS - 1 - turn
        rows = pl.ds(pl.multiple_of(part * chunk, chunk), chunk)
        partial = [
            lax.dot_general(
                x_all[group, :, rows],
                g_all[slot, group],
                (((0,), (0,)), ((), ())),
                preferred_element_type=jnp.float32,
            )
            for group in range(PARTS)
        ]
        largest = jnp.abs(partial[0])
        for group in range(1, PARTS):
            largest = jnp.maximum(largest, jnp.abs(partial[group]))
        lanes = lax.broadcasted_iota(jnp.int32, (chunk, BLOCK), 1)
        gathered = jnp.zeros((chunk, BLOCK), jnp.float32)
        sums = []
        for block in range(blocks):
            cols = slice(block * BLOCK, (block + 1) * BLOCK)
            size = jnp.max(largest[:, cols], axis=1, keepdims=True) + TINY
            gathered = jnp.where(lanes == block, size, gathered)
            inverse = 1.0 / size
            total = None
            for group in range(PARTS):
                term = (partial[group][:, cols] * inverse).astype(jnp.bfloat16).astype(jnp.float32)
                total = term if total is None else total + term
            sums.append(total.astype(jnp.bfloat16))
        for piece in range(chunk // step):
            stacked = jnp.concatenate([one[piece * step : (piece + 1) * step] for one in sums], axis=0)
            mixed = jnp.dot(spread[...], stacked, preferred_element_type=jnp.float32)
            mant[turn, wide(part * chunk + piece * step, step), :] = mixed.astype(jnp.bfloat16)
        scale[turn, :, rows] = jnp.transpose(gathered)[:8, :]

        @pl.when(turn < PARTS - 1)
        def _():
            m_out(turn, part).start()

        @pl.when(turn == PARTS - 1)
        def _():
            m_here(part).start()

        return 0

    lax.fori_loop(0, PARTS * PARTS, weight_step, 0)

    def s_out(turn):
        cols = pl.ds(pl.multiple_of(mp * share, share), share)
        return remote(scale.at[turn], out_scale.at[:, cols], s_send.at[turn], s_recv.at[turn], along_mp(1 + turn))

    for turn in range(PARTS - 1):
        s_out(turn).start()
    s_here = pltpu.make_async_copy(
        scale.at[PARTS - 1], out_scale.at[:, pl.ds(pl.multiple_of(mp * share, share), share)], local_sem.at[3]
    )
    s_here.start()

    lax.fori_loop(PARTS // 2, PARTS, input_step, 0)

    for copy in x_out + gz_out + gl_out:
        copy.wait_send()
    for by in range(1, PARTS):
        gn_copy(by, dp).wait_send()
    for by in range(PARTS):

        @pl.when(wrap(mp - by) != dp)
        def _():
            x_on(by).wait_send()

    for side in range(2):
        for part in range(2):
            g_out(side, part).wait_send()
        g_on(side).wait_send()
    for by in range(1, PARTS):
        for part in range(PARTS):
            w_out(by, part).wait_send()
    for turn in range(PARTS - 1):
        source = wrap(mp - 1 - turn)
        for part in range(PARTS):
            m_out(turn, part).wait_send()
            rows = wide(source * share + part * chunk, chunk)
            remote(
                mant.at[turn, wide(part * chunk, chunk)],
                out_mant.at[rows],
                m_send.at[turn, part],
                m_recv.at[turn, part],
                along_mp(1 + turn),
            ).wait_recv()
        s_out(turn).wait_send()
        cols = pl.ds(pl.multiple_of(source * share, share), share)
        remote(
            scale.at[turn], out_scale.at[:, cols], s_send.at[turn], s_recv.at[turn], along_mp(1 + turn)
        ).wait_recv()
    for part in range(PARTS):
        m_here(part).wait()
    s_here.wait()

    @pl.when(pipe > 0)
    def _():
        for part in range(PARTS):
            p_out(part).wait_send()

    @pl.when(pipe < sections - 1)
    def _():
        for part in range(PARTS):
            p_out(part).wait_recv()

    @pl.when(pipe == sections - 1)
    def _():
        for part in range(PARTS):
            pltpu.make_async_copy(
                zeros, out_grad.at[pl.ds(part * tokens, tokens)], zero_sem.at[part]
            ).wait()


def paired(array):
    count, pair, columns = array.shape
    split = array.reshape(count, pair, columns // BLOCK, BLOCK)
    return split.transpose(0, 2, 1, 3).reshape(-1, BLOCK)


def on_device(sections, layer_input, kv_cotangent, kv_weight):
    features = layer_input[0]
    tokens, width = features.shape
    columns = 2 * kv_cotangent.shape[3]
    rows = kv_weight.shape[1]
    flat_grad = paired(kv_cotangent[0])
    flat_weight = paired(kv_weight[0])
    share = width // PARTS
    blocks = columns // BLOCK
    dma = pltpu.SemaphoreType.DMA
    anywhere = pl.BlockSpec(memory_space=pl.ANY)
    grad, mantissa, scale = pl.pallas_call(
        functools.partial(section_kernel, sections),
        out_shape=(
            jax.ShapeDtypeStruct((tokens * PARTS, share), jnp.bfloat16),
            jax.ShapeDtypeStruct((rows * blocks, BLOCK), jnp.bfloat16),
            jax.ShapeDtypeStruct((8, rows), jnp.float32),
        ),
        in_specs=[anywhere] * 3,
        out_specs=[anywhere] * 3,
        scratch_shapes=[
            pltpu.VMEM((PARTS, tokens, share), jnp.bfloat16),
            pltpu.VMEM((PARTS, tokens, share), jnp.bfloat16),
            pltpu.VMEM((tokens * blocks, BLOCK), jnp.bfloat16),
            pltpu.VMEM((tokens, columns), jnp.bfloat16),
            pltpu.VMEM((rows * blocks, BLOCK), jnp.bfloat16),
            pltpu.VMEM((rows, columns), jnp.bfloat16),
            pltpu.VMEM((SIDE, SIDE), jnp.bfloat16),
            pltpu.VMEM((SIDE, SIDE), jnp.bfloat16),
            pltpu.VMEM((PARTS, PARTS, tokens, columns), jnp.bfloat16),
            pltpu.VMEM((PARTS, share, columns), jnp.bfloat16),
            pltpu.VMEM((PARTS, share * blocks, BLOCK), jnp.bfloat16),
            pltpu.VMEM((PARTS, 8, share), jnp.float32),
            pltpu.VMEM((tokens * PARTS, share), jnp.bfloat16),
            pltpu.VMEM((tokens, share), jnp.bfloat16),
            dma((PARTS,)),
            dma((PARTS,)),
            dma((PARTS,)),
            dma((PARTS,)),
            dma((PARTS,)),
            dma((PARTS,)),
            dma((2, 2)),
            dma((2, 2)),
            dma((2,)),
            dma((2,)),
            dma((PARTS,)),
            dma((PARTS,)),
            dma((PARTS,)),
            dma((PARTS,)),
            dma((PARTS, PARTS)),
            dma((PARTS, PARTS)),
            dma((PARTS, PARTS)),
            dma((PARTS, PARTS)),
            dma((PARTS,)),
            dma((PARTS,)),
            dma((PARTS,)),
            dma((PARTS,)),
            dma((6,)),
            dma((PARTS,)),
            dma((PARTS,)),
        ],
        name="section",
        compiler_params=pltpu.CompilerParams(
            collective_id=0, has_side_effects=True, vmem_limit_bytes=56 << 20
        ),
    )(features, flat_grad, flat_weight)
    mantissa = mantissa.reshape(rows, blocks // 2, 2, BLOCK).transpose(0, 2, 1, 3)
    mantissa = mantissa.reshape(rows, 2, columns // 2)
    scale = scale[:blocks].T.reshape(rows, 2, blocks // 2)
    return grad[None], mantissa[None], scale[None]


def solution(mesh):
    in_specs = (P("pipe", "dp", "mp"), P("pipe", "dp", None, "mp"), P("pipe", "dp", None, "mp"))
    out_specs = (
        P("pipe", None, ("dp", "mp")),
        P("pipe", "dp", None, "mp"),
        P("pipe", "dp", None, "mp"),
    )
    return jax.shard_map(
        functools.partial(on_device, mesh.shape["pipe"]),
        mesh=mesh,
        in_specs=in_specs,
        out_specs=out_specs,
        check_vma=False,
    )
```

```python
import functools

import jax
import jax.numpy as jnp
from jax import lax
from jax.experimental import pallas as pl
from jax.experimental.pallas import tpu as pltpu
from jax.sharding import PartitionSpec as P

BLOCK = 128
SIDE = 256
EARLY = 3
TINY = 1e-6
MESH = pl.DeviceIdType.MESH
PARTS = 4


def wrap(index):
    return lax.rem(index + 2 * PARTS, PARTS)


def section_kernel(
    sections,
    x_ref,
    g_ref,
    w_ref,
    out_grad,
    out_mant,
    out_scale,
    x_stage,
    x_all,
    g_raw,
    w_raw,
    w_own,
    spread,
    gather,
    g_all,
    w_all,
    mant,
    scale,
    made,
    zeros,
    x_send,
    x_recv,
    xz_send,
    xz_recv,
    gz_send,
    gz_recv,
    gy_send,
    gy_recv,
    gf_send,
    gf_recv,
    gl_send,
    gl_recv,
    gn_send,
    gn_recv,
    w_send,
    w_recv,
    m_send,
    m_recv,
    s_send,
    s_recv,
    p_send,
    p_recv,
    local_sem,
    m_local,
    zero_sem,
):
    pipe, dp, mp = lax.axis_index("pipe"), lax.axis_index("dp"), lax.axis_index("mp")
    tokens, features = x_ref.shape
    columns = g_all.shape[3]
    share = features // PARTS
    chunk = share // PARTS
    lead = tokens // 2
    first, last = pl.ds(0, lead), pl.ds(lead, tokens - lead)
    blocks = columns // BLOCK
    step = SIDE // blocks

    def along_mp(by):
        return (pipe, dp, wrap(mp + by))

    def along_dp(to):
        return (pipe, to, mp)

    def remote(src, dst, send, recv, device):
        return pltpu.make_async_remote_copy(
            src_ref=src, dst_ref=dst, send_sem=send, recv_sem=recv, device_id=device, device_id_type=MESH
        )

    g_in = pltpu.make_async_copy(g_ref, g_raw, local_sem.at[4])
    w_in = pltpu.make_async_copy(w_ref, w_raw, local_sem.at[5])
    g_in.start()
    w_in.start()

    barrier = pltpu.get_barrier_semaphore()
    for by in range(1, PARTS):
        pl.semaphore_signal(barrier, inc=1, device_id=along_mp(by), device_id_type=MESH)
        pl.semaphore_signal(barrier, inc=1, device_id=along_dp(wrap(dp + by)), device_id_type=MESH)

    for by in (1, sections - 1):
        pl.semaphore_signal(
            barrier, inc=1, device_id=(lax.rem(pipe + by, sections), dp, mp), device_id_type=MESH
        )

    line = lax.broadcasted_iota(jnp.int32, (SIDE, SIDE), 0)
    column = lax.broadcasted_iota(jnp.int32, (SIDE, SIDE), 1)

    def place(index):
        return (index % 2 * 2 + index // 2 % 2) * step + index // blocks

    spread[...] = jnp.where(column == place(line), 1.0, 0.0).astype(jnp.bfloat16)
    gather[...] = jnp.where(line == place(column), 1.0, 0.0).astype(jnp.bfloat16)

    def untangle(raw, own, index):
        many = pl.ds(pl.multiple_of(index * SIDE, SIDE), SIDE)
        rows = pl.ds(pl.multiple_of(index * step, step), step)
        sorted_rows = jnp.dot(gather[...], raw[many, :], preferred_element_type=jnp.float32)
        for block in range(blocks):
            own[rows, block * BLOCK : (block + 1) * BLOCK] = sorted_rows[
                block * step : (block + 1) * step
            ].astype(jnp.bfloat16)

    g_in.wait()
    for index in range(tokens // step):
        untangle(g_raw, g_all.at[0, dp], index)

    pl.semaphore_wait(barrier, 2 * (PARTS - 1) + 2)

    def quarter(index):
        return pl.ds(pl.multiple_of(index * share, share), share)

    x_out = [
        remote(
            x_ref.at[:, quarter(wrap(mp + by))], x_stage.at[by], x_send.at[by], x_recv.at[by], along_mp(by)
        )
        for by in range(1, PARTS)
    ]
    gl_out = [
        remote(
            g_all.at[0, dp, last], g_all.at[by, dp, last], gl_send.at[by], gl_recv.at[by], along_mp(by)
        )
        for by in range(1, PARTS)
    ]
    GZ, GN = 0, 1

    def block_of(side, back):
        return wrap(dp - back if side == 0 else dp + back)

    def chain(kind, side, turn, back):
        block = block_of(side, back)
        part = g_all.at[0, block, first] if kind == GZ else g_all.at[:, block, last]
        send, recv = (gz_send, gz_recv) if kind == GZ else (gn_send, gn_recv)
        return remote(part, part, send.at[side, turn], recv.at[side, turn], along_dp(block_of(side, -1)))

    def goes(side, turn):
        if side == 0:
            return jnp.logical_and(dp >= turn, dp < PARTS - 1)
        return jnp.logical_and(dp + turn < PARTS, dp > 0)

    def comes(side, turn):
        return dp > turn if side == 0 else dp + turn < PARTS - 1

    def hop(kind, side, turn):
        @pl.when(goes(side, turn))
        def _():
            chain(kind, side, turn, turn).start()

    def arrive(kind, side, turn):
        @pl.when(comes(side, turn))
        def _():
            chain(kind, side, turn, turn + 1).wait_recv()

    def pass_on(kind, turn):
        for side in range(2):
            arrive(kind, side, turn)
            if turn + 1 < PARTS - 1:
                hop(kind, side, turn + 1)

    for copy in gl_out:
        copy.start()
    for side in range(2):
        hop(GZ, side, 0)
    for copy in x_out:
        copy.start()
    own_w = pltpu.make_async_copy(w_own.at[quarter(mp)], w_all.at[0], local_sem.at[1])
    for copy in gl_out:
        copy.wait_recv()
    for side in range(2):
        hop(GN, side, 0)
    w_in.wait()

    def untangle_weights(index, _):
        for part in range(PARTS):
            untangle(w_raw, w_own, index * PARTS + part)
        return 0

    lax.fori_loop(0, share // step, untangle_weights, 0)
    own_w.start()
    pass_on(GZ, 0)
    pass_on(GN, 0)

    def x_from(by):
        return x_ref.at[:, quarter(mp)] if by == 0 else x_stage.at[by]

    def x_on(by):
        owner = wrap(mp - by)
        return remote(x_from(by), x_all.at[dp], xz_send.at[by], xz_recv.at[dp], along_dp(owner))

    for copy in x_out:
        copy.wait_recv()

    def w_out(by, part):
        rows = pl.ds(pl.multiple_of(wrap(mp + by) * share + part * chunk, chunk), chunk)
        return remote(
            w_own.at[rows],
            w_all.at[by, pl.ds(pl.multiple_of(part * chunk, chunk), chunk)],
            w_send.at[by, part],
            w_recv.at[by, part],
            along_mp(by),
        )

    for part in range(EARLY):
        for by in range(1, PARTS):
            w_out(by, part).start()

    pass_on(GZ, 1)
    pass_on(GN, 1)
    for by in range(PARTS):
        @pl.when(wrap(mp - by) != dp)
        def _():
            x_on(by).start()

        @pl.when(wrap(mp - by) == dp)
        def _():
            pltpu.make_async_copy(x_from(by), x_all.at[dp], local_sem.at[2]).start()

    pass_on(GZ, 2)

    def g_half(slot, part):
        return g_all.at[slot, pl.ds(part * (PARTS // 2), PARTS // 2), first]

    def g_out(side, part):
        by, slot = (1, 1) if side == 0 else (-1, 3)
        return remote(
            g_half(0, part), g_half(slot, part), gy_send.at[side, part], gy_recv.at[side, part], along_mp(by)
        )

    def g_on(side):
        by, slot = (1, 1) if side == 0 else (-1, 3)
        return remote(g_half(slot, side), g_half(2, side), gf_send.at[side], gf_recv.at[side], along_mp(by))

    for part in range(2):
        g_out(0, part).start()
        g_out(1, 1 - part).start()

    for side in range(2):
        g_out(side, side).wait_recv()
        g_on(side).start()
    for part in range(EARLY, PARTS):
        for by in range(1, PARTS):
            w_out(by, part).start()

    @pl.when(pipe == sections - 1)
    def _():
        zeros[...] = jnp.zeros_like(zeros)
        for part in range(PARTS):
            pltpu.make_async_copy(
                zeros, out_grad.at[pl.ds(part * tokens, tokens)], zero_sem.at[part]
            ).start()

    for side in range(2):
        g_out(side, 1 - side).wait_recv()
        g_on(side).wait_recv()
    pass_on(GN, 2)
    def p_out(part):
        cols = pl.ds(pl.multiple_of(part * chunk, chunk), chunk)
        before = jnp.maximum(pipe - 1, 0)
        return remote(
            made.at[:, cols], out_grad.at[:, cols], p_send.at[part], p_recv.at[part], (before, dp, mp)
        )

    own_w.wait()

    def input_step(part, _):
        for by in range(1, PARTS):
            w_out(by, part).wait_recv()
        rows = pl.ds(pl.multiple_of(part * chunk, chunk), chunk)

        def token_step(group, _):
            own = pl.ds(pl.multiple_of(group * tokens, tokens), tokens)
            total = None
            for slot in range(PARTS):
                term = lax.dot_general(
                    g_all[slot, group],
                    w_all[slot, rows, :],
                    (((1,), (1,)), ((), ())),
                    preferred_element_type=jnp.float32,
                )
                total = term if total is None else total + term
            made[own, rows] = total.astype(jnp.bfloat16)
            return 0

        lax.fori_loop(0, PARTS, token_step, 0)

        @pl.when(pipe > 0)
        def _():
            p_out(part).start()

        return 0

    lax.fori_loop(0, EARLY, input_step, 0)

    for by in range(1, PARTS):
        source = wrap(dp - by)
        remote(x_stage.at[0], x_all.at[source], xz_send.at[0], xz_recv.at[source], along_dp(source)).wait_recv()
    pltpu.make_async_copy(x_stage.at[0], x_all.at[dp], local_sem.at[2]).wait()

    def wide(first, size):
        return pl.ds(pl.multiple_of(first * blocks, size * blocks), size * blocks)

    def m_out(turn, part):
        rows = wide(mp * share + part * chunk, chunk)
        src = mant.at[turn, wide(part * chunk, chunk)]
        return remote(src, out_mant.at[rows], m_send.at[turn, part], m_recv.at[turn, part], along_mp(1 + turn))

    def m_here(part):
        rows = wide(mp * share + part * chunk, chunk)
        src = mant.at[PARTS - 1, wide(part * chunk, chunk)]
        return pltpu.make_async_copy(src, out_mant.at[rows], m_local.at[part])

    def weight_step(count, _):
        turn, part = count // PARTS, lax.rem(count, PARTS)
        slot = PARTS - 1 - turn
        rows = pl.ds(pl.multiple_of(part * chunk, chunk), chunk)
        partial = [
            lax.dot_general(
                x_all[group, :, rows],
                g_all[slot, group],
                (((0,), (0,)), ((), ())),
                preferred_element_type=jnp.float32,
            )
            for group in range(PARTS)
        ]
        largest = jnp.abs(partial[0])
        for group in range(1, PARTS):
            largest = jnp.maximum(largest, jnp.abs(partial[group]))
        lanes = lax.broadcasted_iota(jnp.int32, (chunk, BLOCK), 1)
        gathered = jnp.zeros((chunk, BLOCK), jnp.float32)
        sums = []
        for block in range(blocks):
            cols = slice(block * BLOCK, (block + 1) * BLOCK)
            size = jnp.max(largest[:, cols], axis=1, keepdims=True) + TINY
            gathered = jnp.where(lanes == block, size, gathered)
            inverse = 1.0 / size
            total = None
            for group in range(PARTS):
                term = (partial[group][:, cols] * inverse).astype(jnp.bfloat16).astype(jnp.float32)
                total = term if total is None else total + term
            sums.append(total.astype(jnp.bfloat16))
        for piece in range(chunk // step):
            stacked = jnp.concatenate([one[piece * step : (piece + 1) * step] for one in sums], axis=0)
            mixed = jnp.dot(spread[...], stacked, preferred_element_type=jnp.float32)
            mant[turn, wide(part * chunk + piece * step, step), :] = mixed.astype(jnp.bfloat16)
        turned = jnp.transpose(gathered)
        for kind in range(2):
            scale[turn, kind, :, rows] = turned[kind * (blocks // 2) : (kind + 1) * (blocks // 2), :]

        @pl.when(turn < PARTS - 1)
        def _():
            m_out(turn, part).start()

        @pl.when(turn == PARTS - 1)
        def _():
            m_here(part).start()

        return 0

    lax.fori_loop(0, PARTS * PARTS, weight_step, 0)

    def s_out(turn):
        cols = pl.ds(pl.multiple_of(mp * share, share), share)
        return remote(scale.at[turn], out_scale.at[:, :, cols], s_send.at[turn], s_recv.at[turn], along_mp(1 + turn))

    for turn in range(PARTS - 1):
        s_out(turn).start()
    s_here = pltpu.make_async_copy(
        scale.at[PARTS - 1], out_scale.at[:, :, pl.ds(pl.multiple_of(mp * share, share), share)], local_sem.at[3]
    )
    s_here.start()

    lax.fori_loop(EARLY, PARTS, input_step, 0)

    for copy in x_out + gl_out:
        copy.wait_send()
    for kind in (GZ, GN):
        for side in range(2):
            for turn in range(PARTS - 1):

                @pl.when(goes(side, turn))
                def _():
                    chain(kind, side, turn, turn).wait_send()

    for by in range(PARTS):

        @pl.when(wrap(mp - by) != dp)
        def _():
            x_on(by).wait_send()

    for side in range(2):
        for part in range(2):
            g_out(side, part).wait_send()
        g_on(side).wait_send()
    for by in range(1, PARTS):
        for part in range(PARTS):
            w_out(by, part).wait_send()
    for turn in range(PARTS - 1):
        source = wrap(mp - 1 - turn)
        for part in range(PARTS):
            m_out(turn, part).wait_send()
            rows = wide(source * share + part * chunk, chunk)
            remote(
                mant.at[turn, wide(part * chunk, chunk)],
                out_mant.at[rows],
                m_send.at[turn, part],
                m_recv.at[turn, part],
                along_mp(1 + turn),
            ).wait_recv()
        s_out(turn).wait_send()
        cols = pl.ds(pl.multiple_of(source * share, share), share)
        remote(
            scale.at[turn], out_scale.at[:, :, cols], s_send.at[turn], s_recv.at[turn], along_mp(1 + turn)
        ).wait_recv()
    for part in range(PARTS):
        m_here(part).wait()
    s_here.wait()

    @pl.when(pipe > 0)
    def _():
        for part in range(PARTS):
            p_out(part).wait_send()

    @pl.when(pipe < sections - 1)
    def _():
        for part in range(PARTS):
            p_out(part).wait_recv()

    @pl.when(pipe == sections - 1)
    def _():
        for part in range(PARTS):
            pltpu.make_async_copy(
                zeros, out_grad.at[pl.ds(part * tokens, tokens)], zero_sem.at[part]
            ).wait()


def paired(array):
    count, pair, columns = array.shape
    split = array.reshape(count, pair, columns // BLOCK, BLOCK)
    return split.transpose(0, 2, 1, 3).reshape(-1, BLOCK)


def on_device(sections, layer_input, kv_cotangent, kv_weight):
    features = layer_input[0]
    tokens, width = features.shape
    columns = 2 * kv_cotangent.shape[3]
    rows = kv_weight.shape[1]
    flat_grad = paired(kv_cotangent[0])
    flat_weight = paired(kv_weight[0])
    share = width // PARTS
    blocks = columns // BLOCK
    dma = pltpu.SemaphoreType.DMA
    anywhere = pl.BlockSpec(memory_space=pl.ANY)
    grad, mantissa, scale = pl.pallas_call(
        functools.partial(section_kernel, sections),
        out_shape=(
            jax.ShapeDtypeStruct((tokens * PARTS, share), jnp.bfloat16),
            jax.ShapeDtypeStruct((rows * blocks, BLOCK), jnp.bfloat16),
            jax.ShapeDtypeStruct((2, blocks // 2, rows), jnp.float32),
        ),
        in_specs=[anywhere] * 3,
        out_specs=[anywhere] * 3,
        scratch_shapes=[
            pltpu.VMEM((PARTS, tokens, share), jnp.bfloat16),
            pltpu.VMEM((PARTS, tokens, share), jnp.bfloat16),
            pltpu.VMEM((tokens * blocks, BLOCK), jnp.bfloat16),
            pltpu.VMEM((rows * blocks, BLOCK), jnp.bfloat16),
            pltpu.VMEM((rows, columns), jnp.bfloat16),
            pltpu.VMEM((SIDE, SIDE), jnp.bfloat16),
            pltpu.VMEM((SIDE, SIDE), jnp.bfloat16),
            pltpu.VMEM((PARTS, PARTS, tokens, columns), jnp.bfloat16),
            pltpu.VMEM((PARTS, share, columns), jnp.bfloat16),
            pltpu.VMEM((PARTS, share * blocks, BLOCK), jnp.bfloat16),
            pltpu.VMEM((PARTS, 2, blocks // 2, share), jnp.float32),
            pltpu.VMEM((tokens * PARTS, share), jnp.bfloat16),
            pltpu.VMEM((tokens, share), jnp.bfloat16),
            dma((PARTS,)),
            dma((PARTS,)),
            dma((PARTS,)),
            dma((PARTS,)),
            dma((2, PARTS)),
            dma((2, PARTS)),
            dma((2, 2)),
            dma((2, 2)),
            dma((2,)),
            dma((2,)),
            dma((PARTS,)),
            dma((PARTS,)),
            dma((2, PARTS)),
            dma((2, PARTS)),
            dma((PARTS, PARTS)),
            dma((PARTS, PARTS)),
            dma((PARTS, PARTS)),
            dma((PARTS, PARTS)),
            dma((PARTS,)),
            dma((PARTS,)),
            dma((PARTS,)),
            dma((PARTS,)),
            dma((6,)),
            dma((PARTS,)),
            dma((PARTS,)),
        ],
        name="section",
        compiler_params=pltpu.CompilerParams(
            collective_id=0, has_side_effects=True, vmem_limit_bytes=56 << 20
        ),
    )(features, flat_grad, flat_weight)
    mantissa = mantissa.reshape(rows, blocks // 2, 2, BLOCK).transpose(0, 2, 1, 3)
    mantissa = mantissa.reshape(rows, 2, columns // 2)
    scale = scale.transpose(2, 0, 1)
    return grad[None], mantissa[None], scale[None]


def solution(mesh):
    in_specs = (P("pipe", "dp", "mp"), P("pipe", "dp", None, "mp"), P("pipe", "dp", None, "mp"))
    out_specs = (
        P("pipe", None, ("dp", "mp")),
        P("pipe", "dp", None, "mp"),
        P("pipe", "dp", None, "mp"),
    )
    return jax.shard_map(
        functools.partial(on_device, mesh.shape["pipe"]),
        mesh=mesh,
        in_specs=in_specs,
        out_specs=out_specs,
        check_vma=False,
    )
```

```python
import functools

import jax
import jax.numpy as jnp
from jax import lax
from jax.experimental import pallas as pl
from jax.experimental.pallas import tpu as pltpu
from jax.sharding import PartitionSpec as P

BLOCK = 128
SIDE = 256
EARLY = 3
TINY = 1e-6
MESH = pl.DeviceIdType.MESH
PARTS = 4


def wrap(index):
    return lax.rem(index + 2 * PARTS, PARTS)


def section_kernel(
    sections,
    x_ref,
    g_ref,
    w_ref,
    out_grad,
    out_mant,
    out_scale,
    x_stage,
    x_all,
    g_raw,
    w_raw,
    w_own,
    spread,
    gather,
    g_all,
    w_all,
    mant,
    scale,
    made,
    zeros,
    x_send,
    x_recv,
    xz_send,
    xz_recv,
    gz_send,
    gz_recv,
    gy_send,
    gy_recv,
    gf_send,
    gf_recv,
    gl_send,
    gl_recv,
    gn_send,
    gn_recv,
    w_send,
    w_recv,
    m_send,
    m_recv,
    s_send,
    s_recv,
    p_send,
    p_recv,
    local_sem,
    m_local,
    zero_sem,
):
    pipe, dp, mp = lax.axis_index("pipe"), lax.axis_index("dp"), lax.axis_index("mp")
    tokens, features = x_ref.shape
    columns = g_all.shape[3]
    share = features // PARTS
    chunk = share // PARTS
    lead = tokens * 7 // 16
    first, last = pl.ds(0, lead), pl.ds(lead, tokens - lead)
    blocks = columns // BLOCK
    step = SIDE // blocks

    def along_mp(by):
        return (pipe, dp, wrap(mp + by))

    def along_dp(to):
        return (pipe, to, mp)

    def remote(src, dst, send, recv, device):
        return pltpu.make_async_remote_copy(
            src_ref=src, dst_ref=dst, send_sem=send, recv_sem=recv, device_id=device, device_id_type=MESH
        )

    g_in = pltpu.make_async_copy(g_ref, g_raw, local_sem.at[4])
    w_in = pltpu.make_async_copy(w_ref, w_raw, local_sem.at[5])
    g_in.start()
    w_in.start()

    barrier = pltpu.get_barrier_semaphore()
    for by in range(1, PARTS):
        pl.semaphore_signal(barrier, inc=1, device_id=along_mp(by), device_id_type=MESH)
        pl.semaphore_signal(barrier, inc=1, device_id=along_dp(wrap(dp + by)), device_id_type=MESH)

    for by in (1, sections - 1):
        pl.semaphore_signal(
            barrier, inc=1, device_id=(lax.rem(pipe + by, sections), dp, mp), device_id_type=MESH
        )

    line = lax.broadcasted_iota(jnp.int32, (SIDE, SIDE), 0)
    column = lax.broadcasted_iota(jnp.int32, (SIDE, SIDE), 1)

    def place(index):
        return (index % 2 * 2 + index // 2 % 2) * step + index // blocks

    spread[...] = jnp.where(column == place(line), 1.0, 0.0).astype(jnp.bfloat16)
    gather[...] = jnp.where(line == place(column), 1.0, 0.0).astype(jnp.bfloat16)

    def untangle(raw, own, index):
        many = pl.ds(pl.multiple_of(index * SIDE, SIDE), SIDE)
        rows = pl.ds(pl.multiple_of(index * step, step), step)
        sorted_rows = jnp.dot(gather[...], raw[many, :], preferred_element_type=jnp.float32)
        for block in range(blocks):
            own[rows, block * BLOCK : (block + 1) * BLOCK] = sorted_rows[
                block * step : (block + 1) * step
            ].astype(jnp.bfloat16)

    g_in.wait()
    for index in range(tokens // step):
        untangle(g_raw, g_all.at[0, dp], index)

    pl.semaphore_wait(barrier, 2 * (PARTS - 1) + 2)

    def quarter(index):
        return pl.ds(pl.multiple_of(index * share, share), share)

    x_out = [
        remote(
            x_ref.at[:, quarter(wrap(mp + by))], x_stage.at[by], x_send.at[by], x_recv.at[by], along_mp(by)
        )
        for by in range(1, PARTS)
    ]
    gl_out = [
        remote(
            g_all.at[0, dp, last], g_all.at[by, dp, last], gl_send.at[by], gl_recv.at[by], along_mp(by)
        )
        for by in range(1, PARTS)
    ]
    GZ, GN = 0, 1

    def block_of(side, back):
        return wrap(dp - back if side == 0 else dp + back)

    def chain(kind, side, turn, back):
        block = block_of(side, back)
        part = g_all.at[0, block, first] if kind == GZ else g_all.at[:, block, last]
        send, recv = (gz_send, gz_recv) if kind == GZ else (gn_send, gn_recv)
        return remote(part, part, send.at[side, turn], recv.at[side, turn], along_dp(block_of(side, -1)))

    def goes(side, turn):
        if side == 0:
            return jnp.logical_and(dp >= turn, dp < PARTS - 1)
        return jnp.logical_and(dp + turn < PARTS, dp > 0)

    def comes(side, turn):
        return dp > turn if side == 0 else dp + turn < PARTS - 1

    def hop(kind, side, turn):
        @pl.when(goes(side, turn))
        def _():
            chain(kind, side, turn, turn).start()

    def arrive(kind, side, turn):
        @pl.when(comes(side, turn))
        def _():
            chain(kind, side, turn, turn + 1).wait_recv()

    def pass_on(kind, turn):
        for side in range(2):
            arrive(kind, side, turn)
            if turn + 1 < PARTS - 1:
                hop(kind, side, turn + 1)

    for copy in gl_out:
        copy.start()
    for side in range(2):
        hop(GZ, side, 0)
    for copy in x_out:
        copy.start()
    own_w = pltpu.make_async_copy(w_own.at[quarter(mp)], w_all.at[0], local_sem.at[1])
    for copy in gl_out:
        copy.wait_recv()
    for side in range(2):
        hop(GN, side, 0)
    w_in.wait()

    def untangle_weights(index, _):
        for part in range(PARTS):
            untangle(w_raw, w_own, index * PARTS + part)
        return 0

    lax.fori_loop(0, share // step, untangle_weights, 0)
    own_w.start()
    pass_on(GZ, 0)
    pass_on(GN, 0)

    def x_from(by):
        return x_ref.at[:, quarter(mp)] if by == 0 else x_stage.at[by]

    def x_on(by):
        owner = wrap(mp - by)
        return remote(x_from(by), x_all.at[dp], xz_send.at[by], xz_recv.at[dp], along_dp(owner))

    for copy in x_out:
        copy.wait_recv()

    def w_out(by, part):
        rows = pl.ds(pl.multiple_of(wrap(mp + by) * share + part * chunk, chunk), chunk)
        return remote(
            w_own.at[rows],
            w_all.at[by, pl.ds(pl.multiple_of(part * chunk, chunk), chunk)],
            w_send.at[by, part],
            w_recv.at[by, part],
            along_mp(by),
        )

    for part in range(EARLY):
        for by in range(1, PARTS):
            w_out(by, part).start()

    pass_on(GZ, 1)
    pass_on(GN, 1)
    for by in range(PARTS):
        @pl.when(wrap(mp - by) != dp)
        def _():
            x_on(by).start()

        @pl.when(wrap(mp - by) == dp)
        def _():
            pltpu.make_async_copy(x_from(by), x_all.at[dp], local_sem.at[2]).start()

    pass_on(GZ, 2)

    def g_half(slot, part):
        return g_all.at[slot, pl.ds(part * (PARTS // 2), PARTS // 2), first]

    def g_out(side, part):
        by, slot = (1, 1) if side == 0 else (-1, 3)
        return remote(
            g_half(0, part), g_half(slot, part), gy_send.at[side, part], gy_recv.at[side, part], along_mp(by)
        )

    def g_on(side):
        by, slot = (1, 1) if side == 0 else (-1, 3)
        return remote(g_half(slot, side), g_half(2, side), gf_send.at[side], gf_recv.at[side], along_mp(by))

    for part in range(2):
        g_out(0, part).start()
        g_out(1, 1 - part).start()

    for side in range(2):
        g_out(side, side).wait_recv()
        g_on(side).start()
    for part in range(EARLY, PARTS):
        for by in range(1, PARTS):
            w_out(by, part).start()

    @pl.when(pipe == sections - 1)
    def _():
        zeros[...] = jnp.zeros_like(zeros)
        for part in range(PARTS):
            pltpu.make_async_copy(
                zeros, out_grad.at[pl.ds(part * tokens, tokens)], zero_sem.at[part]
            ).start()

    for side in range(2):
        g_out(side, 1 - side).wait_recv()
        g_on(side).wait_recv()
    pass_on(GN, 2)
    def p_out(part):
        cols = pl.ds(pl.multiple_of(part * chunk, chunk), chunk)
        before = jnp.maximum(pipe - 1, 0)
        return remote(
            made.at[:, cols], out_grad.at[:, cols], p_send.at[part], p_recv.at[part], (before, dp, mp)
        )

    own_w.wait()

    def input_step(part, _):
        for by in range(1, PARTS):
            w_out(by, part).wait_recv()
        rows = pl.ds(pl.multiple_of(part * chunk, chunk), chunk)

        def token_step(group, _):
            own = pl.ds(pl.multiple_of(group * tokens, tokens), tokens)
            total = None
            for slot in range(PARTS):
                term = lax.dot_general(
                    g_all[slot, group],
                    w_all[slot, rows, :],
                    (((1,), (1,)), ((), ())),
                    preferred_element_type=jnp.float32,
                )
                total = term if total is None else total + term
            made[own, rows] = total.astype(jnp.bfloat16)
            return 0

        lax.fori_loop(0, PARTS, token_step, 0)

        @pl.when(pipe > 0)
        def _():
            p_out(part).start()

        return 0

    lax.fori_loop(0, EARLY, input_step, 0)

    for by in range(1, PARTS):
        source = wrap(dp - by)
        remote(x_stage.at[0], x_all.at[source], xz_send.at[0], xz_recv.at[source], along_dp(source)).wait_recv()
    pltpu.make_async_copy(x_stage.at[0], x_all.at[dp], local_sem.at[2]).wait()

    def wide(first, size):
        return pl.ds(pl.multiple_of(first * blocks, size * blocks), size * blocks)

    def m_out(turn, part):
        rows = wide(mp * share + part * chunk, chunk)
        src = mant.at[turn, wide(part * chunk, chunk)]
        return remote(src, out_mant.at[rows], m_send.at[turn, part], m_recv.at[turn, part], along_mp(1 + turn))

    def m_here(part):
        rows = wide(mp * share + part * chunk, chunk)
        src = mant.at[PARTS - 1, wide(part * chunk, chunk)]
        return pltpu.make_async_copy(src, out_mant.at[rows], m_local.at[part])

    def weight_step(count, _):
        turn, part = count // PARTS, lax.rem(count, PARTS)
        slot = PARTS - 1 - turn
        rows = pl.ds(pl.multiple_of(part * chunk, chunk), chunk)
        partial = [
            lax.dot_general(
                x_all[group, :, rows],
                g_all[slot, group],
                (((0,), (0,)), ((), ())),
                preferred_element_type=jnp.float32,
            )
            for group in range(PARTS)
        ]
        largest = jnp.abs(partial[0])
        for group in range(1, PARTS):
            largest = jnp.maximum(largest, jnp.abs(partial[group]))
        lanes = lax.broadcasted_iota(jnp.int32, (chunk, BLOCK), 1)
        gathered = jnp.zeros((chunk, BLOCK), jnp.float32)
        sums = []
        for block in range(blocks):
            cols = slice(block * BLOCK, (block + 1) * BLOCK)
            size = jnp.max(largest[:, cols], axis=1, keepdims=True) + TINY
            gathered = jnp.where(lanes == block, size, gathered)
            inverse = 1.0 / size
            total = None
            for group in range(PARTS):
                term = (partial[group][:, cols] * inverse).astype(jnp.bfloat16).astype(jnp.float32)
                total = term if total is None else total + term
            sums.append(total.astype(jnp.bfloat16))
        for piece in range(chunk // step):
            stacked = jnp.concatenate([one[piece * step : (piece + 1) * step] for one in sums], axis=0)
            mixed = jnp.dot(spread[...], stacked, preferred_element_type=jnp.float32)
            mant[turn, wide(part * chunk + piece * step, step), :] = mixed.astype(jnp.bfloat16)
        turned = jnp.transpose(gathered)
        for kind in range(2):
            scale[turn, kind, :, rows] = turned[kind * (blocks // 2) : (kind + 1) * (blocks // 2), :]

        @pl.when(turn < PARTS - 1)
        def _():
            m_out(turn, part).start()

        @pl.when(turn == PARTS - 1)
        def _():
            m_here(part).start()

        return 0

    lax.fori_loop(0, PARTS * PARTS, weight_step, 0)

    def s_out(turn):
        cols = pl.ds(pl.multiple_of(mp * share, share), share)
        return remote(scale.at[turn], out_scale.at[:, :, cols], s_send.at[turn], s_recv.at[turn], along_mp(1 + turn))

    for turn in range(PARTS - 1):
        s_out(turn).start()
    s_here = pltpu.make_async_copy(
        scale.at[PARTS - 1], out_scale.at[:, :, pl.ds(pl.multiple_of(mp * share, share), share)], local_sem.at[3]
    )
    s_here.start()

    lax.fori_loop(EARLY, PARTS, input_step, 0)

    for copy in x_out + gl_out:
        copy.wait_send()
    for kind in (GZ, GN):
        for side in range(2):
            for turn in range(PARTS - 1):

                @pl.when(goes(side, turn))
                def _():
                    chain(kind, side, turn, turn).wait_send()

    for by in range(PARTS):

        @pl.when(wrap(mp - by) != dp)
        def _():
            x_on(by).wait_send()

    for side in range(2):
        for part in range(2):
            g_out(side, part).wait_send()
        g_on(side).wait_send()
    for by in range(1, PARTS):
        for part in range(PARTS):
            w_out(by, part).wait_send()
    for turn in range(PARTS - 1):
        source = wrap(mp - 1 - turn)
        for part in range(PARTS):
            m_out(turn, part).wait_send()
            rows = wide(source * share + part * chunk, chunk)
            remote(
                mant.at[turn, wide(part * chunk, chunk)],
                out_mant.at[rows],
                m_send.at[turn, part],
                m_recv.at[turn, part],
                along_mp(1 + turn),
            ).wait_recv()
        s_out(turn).wait_send()
        cols = pl.ds(pl.multiple_of(source * share, share), share)
        remote(
            scale.at[turn], out_scale.at[:, :, cols], s_send.at[turn], s_recv.at[turn], along_mp(1 + turn)
        ).wait_recv()
    for part in range(PARTS):
        m_here(part).wait()
    s_here.wait()

    @pl.when(pipe > 0)
    def _():
        for part in range(PARTS):
            p_out(part).wait_send()

    @pl.when(pipe < sections - 1)
    def _():
        for part in range(PARTS):
            p_out(part).wait_recv()

    @pl.when(pipe == sections - 1)
    def _():
        for part in range(PARTS):
            pltpu.make_async_copy(
                zeros, out_grad.at[pl.ds(part * tokens, tokens)], zero_sem.at[part]
            ).wait()


def paired(array):
    count, pair, columns = array.shape
    split = array.reshape(count, pair, columns // BLOCK, BLOCK)
    return split.transpose(0, 2, 1, 3).reshape(-1, BLOCK)


def on_device(sections, layer_input, kv_cotangent, kv_weight):
    features = layer_input[0]
    tokens, width = features.shape
    columns = 2 * kv_cotangent.shape[3]
    rows = kv_weight.shape[1]
    flat_grad = paired(kv_cotangent[0])
    flat_weight = paired(kv_weight[0])
    share = width // PARTS
    blocks = columns // BLOCK
    dma = pltpu.SemaphoreType.DMA
    anywhere = pl.BlockSpec(memory_space=pl.ANY)
    grad, mantissa, scale = pl.pallas_call(
        functools.partial(section_kernel, sections),
        out_shape=(
            jax.ShapeDtypeStruct((tokens * PARTS, share), jnp.bfloat16),
            jax.ShapeDtypeStruct((rows * blocks, BLOCK), jnp.bfloat16),
            jax.ShapeDtypeStruct((2, blocks // 2, rows), jnp.float32),
        ),
        in_specs=[anywhere] * 3,
        out_specs=[anywhere] * 3,
        scratch_shapes=[
            pltpu.VMEM((PARTS, tokens, share), jnp.bfloat16),
            pltpu.VMEM((PARTS, tokens, share), jnp.bfloat16),
            pltpu.VMEM((tokens * blocks, BLOCK), jnp.bfloat16),
            pltpu.VMEM((rows * blocks, BLOCK), jnp.bfloat16),
            pltpu.VMEM((rows, columns), jnp.bfloat16),
            pltpu.VMEM((SIDE, SIDE), jnp.bfloat16),
            pltpu.VMEM((SIDE, SIDE), jnp.bfloat16),
            pltpu.VMEM((PARTS, PARTS, tokens, columns), jnp.bfloat16),
            pltpu.VMEM((PARTS, share, columns), jnp.bfloat16),
            pltpu.VMEM((PARTS, share * blocks, BLOCK), jnp.bfloat16),
            pltpu.VMEM((PARTS, 2, blocks // 2, share), jnp.float32),
            pltpu.VMEM((tokens * PARTS, share), jnp.bfloat16),
            pltpu.VMEM((tokens, share), jnp.bfloat16),
            dma((PARTS,)),
            dma((PARTS,)),
            dma((PARTS,)),
            dma((PARTS,)),
            dma((2, PARTS)),
            dma((2, PARTS)),
            dma((2, 2)),
            dma((2, 2)),
            dma((2,)),
            dma((2,)),
            dma((PARTS,)),
            dma((PARTS,)),
            dma((2, PARTS)),
            dma((2, PARTS)),
            dma((PARTS, PARTS)),
            dma((PARTS, PARTS)),
            dma((PARTS, PARTS)),
            dma((PARTS, PARTS)),
            dma((PARTS,)),
            dma((PARTS,)),
            dma((PARTS,)),
            dma((PARTS,)),
            dma((6,)),
            dma((PARTS,)),
            dma((PARTS,)),
        ],
        name="section",
        compiler_params=pltpu.CompilerParams(
            collective_id=0, has_side_effects=True, vmem_limit_bytes=56 << 20
        ),
    )(features, flat_grad, flat_weight)
    mantissa = mantissa.reshape(rows, blocks // 2, 2, BLOCK).transpose(0, 2, 1, 3)
    mantissa = mantissa.reshape(rows, 2, columns // 2)
    scale = scale.transpose(2, 0, 1)
    return grad[None], mantissa[None], scale[None]


def solution(mesh):
    in_specs = (P("pipe", "dp", "mp"), P("pipe", "dp", None, "mp"), P("pipe", "dp", None, "mp"))
    out_specs = (
        P("pipe", None, ("dp", "mp")),
        P("pipe", "dp", None, "mp"),
        P("pipe", "dp", None, "mp"),
    )
    return jax.shard_map(
        functools.partial(on_device, mesh.shape["pipe"]),
        mesh=mesh,
        in_specs=in_specs,
        out_specs=out_specs,
        check_vma=False,
    )
```

```python
import functools

import jax
import jax.numpy as jnp
from jax import lax
from jax.experimental import pallas as pl
from jax.experimental.pallas import tpu as pltpu
from jax.sharding import PartitionSpec as P

BLOCK = 128
SIDE = 256
EARLY = 3
TINY = 1e-6
MESH = pl.DeviceIdType.MESH
PARTS = 4


def wrap(index):
    return lax.rem(index + 2 * PARTS, PARTS)


def section_kernel(
    sections,
    x_ref,
    g_ref,
    w_ref,
    out_grad,
    out_mant,
    out_scale,
    x_stage,
    x_all,
    g_raw,
    w_raw,
    w_own,
    spread,
    gather,
    g_all,
    w_all,
    mant,
    scale,
    made,
    zeros,
    x_send,
    x_recv,
    xz_send,
    xz_recv,
    gz_send,
    gz_recv,
    gy_send,
    gy_recv,
    gf_send,
    gf_recv,
    gl_send,
    gl_recv,
    gn_send,
    gn_recv,
    w_send,
    w_recv,
    m_send,
    m_recv,
    s_send,
    s_recv,
    p_send,
    p_recv,
    local_sem,
    m_local,
    zero_sem,
):
    pipe, dp, mp = lax.axis_index("pipe"), lax.axis_index("dp"), lax.axis_index("mp")
    tokens, features = x_ref.shape
    columns = g_all.shape[3]
    share = features // PARTS
    chunk = share // PARTS
    lead = tokens * 7 // 16
    first, last = pl.ds(0, lead), pl.ds(lead, tokens - lead)
    blocks = columns // BLOCK
    step = SIDE // blocks

    def along_mp(by):
        return (pipe, dp, wrap(mp + by))

    def along_dp(to):
        return (pipe, to, mp)

    def remote(src, dst, send, recv, device):
        return pltpu.make_async_remote_copy(
            src_ref=src, dst_ref=dst, send_sem=send, recv_sem=recv, device_id=device, device_id_type=MESH
        )

    g_in = pltpu.make_async_copy(g_ref, g_raw, local_sem.at[4])
    w_in = pltpu.make_async_copy(w_ref, w_raw, local_sem.at[5])
    g_in.start()
    w_in.start()

    barrier = pltpu.get_barrier_semaphore()
    for by in range(1, PARTS):
        pl.semaphore_signal(barrier, inc=1, device_id=along_mp(by), device_id_type=MESH)
        pl.semaphore_signal(barrier, inc=1, device_id=along_dp(wrap(dp + by)), device_id_type=MESH)

    for by in (1, sections - 1):
        pl.semaphore_signal(
            barrier, inc=1, device_id=(lax.rem(pipe + by, sections), dp, mp), device_id_type=MESH
        )

    line = lax.broadcasted_iota(jnp.int32, (SIDE, SIDE), 0)
    column = lax.broadcasted_iota(jnp.int32, (SIDE, SIDE), 1)

    def place(index):
        return (index % 2 * 2 + index // 2 % 2) * step + index // blocks

    spread[...] = jnp.where(column == place(line), 1.0, 0.0).astype(jnp.bfloat16)
    gather[...] = jnp.where(line == place(column), 1.0, 0.0).astype(jnp.bfloat16)

    def untangle(raw, own, index):
        many = pl.ds(pl.multiple_of(index * SIDE, SIDE), SIDE)
        rows = pl.ds(pl.multiple_of(index * step, step), step)
        sorted_rows = jnp.dot(gather[...], raw[many, :], preferred_element_type=jnp.float32)
        for block in range(blocks):
            own[rows, block * BLOCK : (block + 1) * BLOCK] = sorted_rows[
                block * step : (block + 1) * step
            ].astype(jnp.bfloat16)

    g_in.wait()
    for index in range(tokens // step):
        untangle(g_raw, g_all.at[0, dp], index)

    pl.semaphore_wait(barrier, 2 * (PARTS - 1) + 2)

    def quarter(index):
        return pl.ds(pl.multiple_of(index * share, share), share)

    x_out = [
        remote(
            x_ref.at[:, quarter(wrap(mp + by))], x_stage.at[by], x_send.at[by], x_recv.at[by], along_mp(by)
        )
        for by in range(1, PARTS)
    ]
    gl_out = [
        remote(
            g_all.at[0, dp, last], g_all.at[by, dp, last], gl_send.at[by], gl_recv.at[by], along_mp(by)
        )
        for by in range(1, PARTS)
    ]
    GZ, GN = 0, 1

    def block_of(side, back):
        return wrap(dp - back if side == 0 else dp + back)

    def chain(kind, side, turn, back):
        block = block_of(side, back)
        part = g_all.at[0, block, first] if kind == GZ else g_all.at[:, block, last]
        send, recv = (gz_send, gz_recv) if kind == GZ else (gn_send, gn_recv)
        return remote(part, part, send.at[side, turn], recv.at[side, turn], along_dp(block_of(side, -1)))

    def goes(side, turn):
        if side == 0:
            return jnp.logical_and(dp >= turn, dp < PARTS - 1)
        return jnp.logical_and(dp + turn < PARTS, dp > 0)

    def comes(side, turn):
        return dp > turn if side == 0 else dp + turn < PARTS - 1

    def hop(kind, side, turn):
        @pl.when(goes(side, turn))
        def _():
            chain(kind, side, turn, turn).start()

    def arrive(kind, side, turn):
        @pl.when(comes(side, turn))
        def _():
            chain(kind, side, turn, turn + 1).wait_recv()

    def pass_on(kind, turn):
        for side in range(2):
            arrive(kind, side, turn)
            if turn + 1 < PARTS - 1:
                hop(kind, side, turn + 1)

    for copy in gl_out:
        copy.start()
    for side in range(2):
        hop(GZ, side, 0)
    for copy in x_out:
        copy.start()
    own_w = pltpu.make_async_copy(w_own.at[quarter(mp)], w_all.at[0], local_sem.at[1])
    for copy in gl_out:
        copy.wait_recv()
    for side in range(2):
        hop(GN, side, 0)
    w_in.wait()

    def untangle_weights(index, _):
        for part in range(PARTS):
            untangle(w_raw, w_own, index * PARTS + part)
        return 0

    lax.fori_loop(0, share // step, untangle_weights, 0)
    own_w.start()
    pass_on(GZ, 0)
    pass_on(GN, 0)

    def x_from(by):
        return x_ref.at[:, quarter(mp)] if by == 0 else x_stage.at[by]

    def x_on(by):
        owner = wrap(mp - by)
        return remote(x_from(by), x_all.at[dp], xz_send.at[by], xz_recv.at[dp], along_dp(owner))

    for copy in x_out:
        copy.wait_recv()

    def w_out(by, part):
        rows = pl.ds(pl.multiple_of(wrap(mp + by) * share + part * chunk, chunk), chunk)
        return remote(
            w_own.at[rows],
            w_all.at[by, pl.ds(pl.multiple_of(part * chunk, chunk), chunk)],
            w_send.at[by, part],
            w_recv.at[by, part],
            along_mp(by),
        )

    for part in range(EARLY):
        for by in range(1, PARTS):
            w_out(by, part).start()

    pass_on(GZ, 1)
    pass_on(GN, 1)
    for by in range(PARTS):
        @pl.when(wrap(mp - by) != dp)
        def _():
            x_on(by).start()

        @pl.when(wrap(mp - by) == dp)
        def _():
            pltpu.make_async_copy(x_from(by), x_all.at[dp], local_sem.at[2]).start()

    pass_on(GZ, 2)

    def g_half(slot, part):
        return g_all.at[slot, pl.ds(part * (PARTS // 2), PARTS // 2), first]

    def g_out(side, part):
        by, slot = (1, 1) if side == 0 else (-1, 3)
        return remote(
            g_half(0, part), g_half(slot, part), gy_send.at[side, part], gy_recv.at[side, part], along_mp(by)
        )

    def g_on(side):
        by, slot = (1, 1) if side == 0 else (-1, 3)
        return remote(g_half(slot, side), g_half(2, side), gf_send.at[side], gf_recv.at[side], along_mp(by))

    for part in range(2):
        g_out(0, part).start()
        g_out(1, 1 - part).start()

    for side in range(2):
        g_out(side, side).wait_recv()
        g_on(side).start()
    for part in range(EARLY, PARTS):
        for by in range(1, PARTS):
            w_out(by, part).start()

    @pl.when(pipe == sections - 1)
    def _():
        zeros[...] = jnp.zeros_like(zeros)
        for part in range(PARTS):
            pltpu.make_async_copy(
                zeros, out_grad.at[pl.ds(part * tokens, tokens)], zero_sem.at[part]
            ).start()

    for side in range(2):
        g_out(side, 1 - side).wait_recv()
        g_on(side).wait_recv()
    pass_on(GN, 2)
    def p_out(part):
        cols = pl.ds(pl.multiple_of(part * chunk, chunk), chunk)
        before = jnp.maximum(pipe - 1, 0)
        return remote(
            made.at[:, cols], out_grad.at[:, cols], p_send.at[part], p_recv.at[part], (before, dp, mp)
        )

    own_w.wait()

    def input_step(part, _):
        for by in range(1, PARTS):
            w_out(by, part).wait_recv()
        rows = pl.ds(pl.multiple_of(part * chunk, chunk), chunk)

        def token_step(group, _):
            own = pl.ds(pl.multiple_of(group * tokens, tokens), tokens)
            total = None
            for slot in range(PARTS):
                term = lax.dot_general(
                    g_all[slot, group],
                    w_all[slot, rows, :],
                    (((1,), (1,)), ((), ())),
                    preferred_element_type=jnp.float32,
                )
                total = term if total is None else total + term
            made[own, rows] = total.astype(jnp.bfloat16)
            return 0

        lax.fori_loop(0, PARTS, token_step, 0)

        @pl.when(pipe > 0)
        def _():
            p_out(part).start()

        return 0

    lax.fori_loop(0, EARLY, input_step, 0)

    for by in range(1, PARTS):
        source = wrap(dp - by)
        remote(x_stage.at[0], x_all.at[source], xz_send.at[0], xz_recv.at[source], along_dp(source)).wait_recv()
    pltpu.make_async_copy(x_stage.at[0], x_all.at[dp], local_sem.at[2]).wait()

    def reach(turn):
        return 2 - turn + 3 * (turn // 2) + 2 * (turn // 3)

    def wide(first, size):
        return pl.ds(pl.multiple_of(first * blocks, size * blocks), size * blocks)

    def m_out(turn, part):
        rows = wide(mp * share + part * chunk, chunk)
        src = mant.at[turn, wide(part * chunk, chunk)]
        return remote(src, out_mant.at[rows], m_send.at[turn, part], m_recv.at[turn, part], along_mp(reach(turn)))

    def m_here(part):
        rows = wide(mp * share + part * chunk, chunk)
        src = mant.at[PARTS - 1, wide(part * chunk, chunk)]
        return pltpu.make_async_copy(src, out_mant.at[rows], m_local.at[part])

    def weight_step(count, _):
        turn, part = count // PARTS, lax.rem(count, PARTS)
        slot = PARTS - reach(turn)
        rows = pl.ds(pl.multiple_of(part * chunk, chunk), chunk)
        partial = [
            lax.dot_general(
                x_all[group, :, rows],
                g_all[slot, group],
                (((0,), (0,)), ((), ())),
                preferred_element_type=jnp.float32,
            )
            for group in range(PARTS)
        ]
        largest = jnp.abs(partial[0])
        for group in range(1, PARTS):
            largest = jnp.maximum(largest, jnp.abs(partial[group]))
        lanes = lax.broadcasted_iota(jnp.int32, (chunk, BLOCK), 1)
        gathered = jnp.zeros((chunk, BLOCK), jnp.float32)
        sums = []
        for block in range(blocks):
            cols = slice(block * BLOCK, (block + 1) * BLOCK)
            size = jnp.max(largest[:, cols], axis=1, keepdims=True) + TINY
            gathered = jnp.where(lanes == block, size, gathered)
            inverse = 1.0 / size
            total = None
            for group in range(PARTS):
                term = (partial[group][:, cols] * inverse).astype(jnp.bfloat16).astype(jnp.float32)
                total = term if total is None else total + term
            sums.append(total.astype(jnp.bfloat16))
        for piece in range(chunk // step):
            stacked = jnp.concatenate([one[piece * step : (piece + 1) * step] for one in sums], axis=0)
            mixed = jnp.dot(spread[...], stacked, preferred_element_type=jnp.float32)
            mant[turn, wide(part * chunk + piece * step, step), :] = mixed.astype(jnp.bfloat16)
        turned = jnp.transpose(gathered)
        for kind in range(2):
            scale[turn, kind, :, rows] = turned[kind * (blocks // 2) : (kind + 1) * (blocks // 2), :]

        @pl.when(turn < PARTS - 1)
        def _():
            m_out(turn, part).start()

        @pl.when(turn == PARTS - 1)
        def _():
            m_here(part).start()

        return 0

    lax.fori_loop(0, PARTS * PARTS, weight_step, 0)

    def s_out(turn):
        cols = pl.ds(pl.multiple_of(mp * share, share), share)
        return remote(scale.at[turn], out_scale.at[:, :, cols], s_send.at[turn], s_recv.at[turn], along_mp(reach(turn)))

    for turn in range(PARTS - 1):
        s_out(turn).start()
    s_here = pltpu.make_async_copy(
        scale.at[PARTS - 1], out_scale.at[:, :, pl.ds(pl.multiple_of(mp * share, share), share)], local_sem.at[3]
    )
    s_here.start()

    lax.fori_loop(EARLY, PARTS, input_step, 0)

    for copy in x_out + gl_out:
        copy.wait_send()
    for kind in (GZ, GN):
        for side in range(2):
            for turn in range(PARTS - 1):

                @pl.when(goes(side, turn))
                def _():
                    chain(kind, side, turn, turn).wait_send()

    for by in range(PARTS):

        @pl.when(wrap(mp - by) != dp)
        def _():
            x_on(by).wait_send()

    for side in range(2):
        for part in range(2):
            g_out(side, part).wait_send()
        g_on(side).wait_send()
    for by in range(1, PARTS):
        for part in range(PARTS):
            w_out(by, part).wait_send()
    for turn in range(PARTS - 1):
        source = wrap(mp - reach(turn))
        for part in range(PARTS):
            m_out(turn, part).wait_send()
            rows = wide(source * share + part * chunk, chunk)
            remote(
                mant.at[turn, wide(part * chunk, chunk)],
                out_mant.at[rows],
                m_send.at[turn, part],
                m_recv.at[turn, part],
                along_mp(reach(turn)),
            ).wait_recv()
        s_out(turn).wait_send()
        cols = pl.ds(pl.multiple_of(source * share, share), share)
        remote(
            scale.at[turn], out_scale.at[:, :, cols], s_send.at[turn], s_recv.at[turn], along_mp(reach(turn))
        ).wait_recv()
    for part in range(PARTS):
        m_here(part).wait()
    s_here.wait()

    @pl.when(pipe > 0)
    def _():
        for part in range(PARTS):
            p_out(part).wait_send()

    @pl.when(pipe < sections - 1)
    def _():
        for part in range(PARTS):
            p_out(part).wait_recv()

    @pl.when(pipe == sections - 1)
    def _():
        for part in range(PARTS):
            pltpu.make_async_copy(
                zeros, out_grad.at[pl.ds(part * tokens, tokens)], zero_sem.at[part]
            ).wait()


def paired(array):
    count, pair, columns = array.shape
    split = array.reshape(count, pair, columns // BLOCK, BLOCK)
    return split.transpose(0, 2, 1, 3).reshape(-1, BLOCK)


def on_device(sections, layer_input, kv_cotangent, kv_weight):
    features = layer_input[0]
    tokens, width = features.shape
    columns = 2 * kv_cotangent.shape[3]
    rows = kv_weight.shape[1]
    flat_grad = paired(kv_cotangent[0])
    flat_weight = paired(kv_weight[0])
    share = width // PARTS
    blocks = columns // BLOCK
    dma = pltpu.SemaphoreType.DMA
    anywhere = pl.BlockSpec(memory_space=pl.ANY)
    grad, mantissa, scale = pl.pallas_call(
        functools.partial(section_kernel, sections),
        out_shape=(
            jax.ShapeDtypeStruct((tokens * PARTS, share), jnp.bfloat16),
            jax.ShapeDtypeStruct((rows * blocks, BLOCK), jnp.bfloat16),
            jax.ShapeDtypeStruct((2, blocks // 2, rows), jnp.float32),
        ),
        in_specs=[anywhere] * 3,
        out_specs=[anywhere] * 3,
        scratch_shapes=[
            pltpu.VMEM((PARTS, tokens, share), jnp.bfloat16),
            pltpu.VMEM((PARTS, tokens, share), jnp.bfloat16),
            pltpu.VMEM((tokens * blocks, BLOCK), jnp.bfloat16),
            pltpu.VMEM((rows * blocks, BLOCK), jnp.bfloat16),
            pltpu.VMEM((rows, columns), jnp.bfloat16),
            pltpu.VMEM((SIDE, SIDE), jnp.bfloat16),
            pltpu.VMEM((SIDE, SIDE), jnp.bfloat16),
            pltpu.VMEM((PARTS, PARTS, tokens, columns), jnp.bfloat16),
            pltpu.VMEM((PARTS, share, columns), jnp.bfloat16),
            pltpu.VMEM((PARTS, share * blocks, BLOCK), jnp.bfloat16),
            pltpu.VMEM((PARTS, 2, blocks // 2, share), jnp.float32),
            pltpu.VMEM((tokens * PARTS, share), jnp.bfloat16),
            pltpu.VMEM((tokens, share), jnp.bfloat16),
            dma((PARTS,)),
            dma((PARTS,)),
            dma((PARTS,)),
            dma((PARTS,)),
            dma((2, PARTS)),
            dma((2, PARTS)),
            dma((2, 2)),
            dma((2, 2)),
            dma((2,)),
            dma((2,)),
            dma((PARTS,)),
            dma((PARTS,)),
            dma((2, PARTS)),
            dma((2, PARTS)),
            dma((PARTS, PARTS)),
            dma((PARTS, PARTS)),
            dma((PARTS, PARTS)),
            dma((PARTS, PARTS)),
            dma((PARTS,)),
            dma((PARTS,)),
            dma((PARTS,)),
            dma((PARTS,)),
            dma((6,)),
            dma((PARTS,)),
            dma((PARTS,)),
        ],
        name="section",
        compiler_params=pltpu.CompilerParams(
            collective_id=0, has_side_effects=True, vmem_limit_bytes=56 << 20
        ),
    )(features, flat_grad, flat_weight)
    mantissa = mantissa.reshape(rows, blocks // 2, 2, BLOCK).transpose(0, 2, 1, 3)
    mantissa = mantissa.reshape(rows, 2, columns // 2)
    scale = scale.transpose(2, 0, 1)
    return grad[None], mantissa[None], scale[None]


def solution(mesh):
    in_specs = (P("pipe", "dp", "mp"), P("pipe", "dp", None, "mp"), P("pipe", "dp", None, "mp"))
    out_specs = (
        P("pipe", None, ("dp", "mp")),
        P("pipe", "dp", None, "mp"),
        P("pipe", "dp", None, "mp"),
    )
    return jax.shard_map(
        functools.partial(on_device, mesh.shape["pipe"]),
        mesh=mesh,
        in_specs=in_specs,
        out_specs=out_specs,
        check_vma=False,
    )
```
